32 devices in a mesh: tm: 8 (over z, x), head: 4 (over y, core).
Axes of the slice: x: 2, y: 2, z: 4, core: 2. Of those that a mesh axis runs over, the one named last changes fastest.
Arguments:
- query_rows: float32 [8192, 2048], P('tm', 'head'), may hold values from -0.125 to 0.125
- key_rows: float32 [8192, 2048], P('tm', 'head'), may hold values from -0.125 to 0.125
- value_rows: float32 [8192, 2048], P('tm', 'head'), may hold values from -1.25 to 1.25
- out_grad: float32 [8192, 2048], P('tm', 'head'), may hold values from -1.25 to 1.25
- level_weights: float32 [14, 8192], P(None, 'tm'), may hold values from 0.3 to 3
Outputs:
- query_grad: float32 [8192, 2048], P('tm', 'head')
- key_grad: float32 [8192, 2048], P('tm', 'head')
- value_grad: float32 [8192, 2048], P('tm', 'head')
- weight_grad: float32 [14, 8192], P(None, 'tm')
The draws below stay inside these ranges and needn't reach their ends.
All inputs are finite; a program needn't handle non-finite values.
Results may differ from the reference program's by a relative error of at most 0.00011.
Values sent between devices are 32-bit elements; how exact they have to be, the bound alone decides.
No kernel may reach another device: no remote copies, remote signals or barrier semaphores. Data moves between devices by JAX's collectives and lax.ppermute only.
A program may use at most 128 MiB of HBM per device.

```python
import math
import jax
import jax.numpy as jnp
from jax import lax

DK = 128
HEADS = 16
F = 1024
SEQ = 8192
LEV_FR = 10
LEV_TM = 3
LEVELS = 14
N_TM = 8


def level_of(own_key, extent, split, smallest, high):
    loudness = 1.0
    for dim, shards_of in split:
        steps = jax.random.uniform(jax.random.fold_in(jax.random.fold_in(own_key, 6), dim), (shards_of,), jnp.float32, smallest / len(split), high / len(split))
        loudness = loudness * jnp.repeat(jnp.exp(steps), extent[dim] // shards_of).reshape((-1,) + (1,) * (len(extent) - 1 - dim))
    return loudness


def normal_values(rng, shape, deviation, most, shards=(), kind=jnp.bfloat16):
    level = level_of(rng, shape, shards, -0.22, 0.18) if shards else 1.0
    result = jax.random.normal(rng, shape, jnp.float32) * deviation * level
    return jnp.minimum(jnp.maximum(result, -most), most).astype(kind)


def setup_inputs(seed: int = 0) -> dict:
    key_list = jax.random.split(jax.random.key(seed), 6)
    query_rows = normal_values(key_list[0], (SEQ, HEADS * DK), (DK ** -0.5 * SEQ ** -0.16667), 0.125, ((0, 8), (1, 4)), jnp.float32)
    key_rows = normal_values(key_list[1], (SEQ, HEADS * DK), (DK ** -0.5 * SEQ ** -0.16667), 0.125, ((0, 8), (1, 4)), jnp.float32)
    value_rows = normal_values(key_list[2], (SEQ, HEADS * DK), (SEQ ** -0.16667), 1.25, ((0, 8), (1, 4)), jnp.float32)
    out_grad = normal_values(key_list[3], (SEQ, HEADS * DK), (SEQ ** -0.16667), 1.25, ((0, 8), (1, 4)), jnp.float32)
    level_weights = jnp.clip(jnp.exp(math.log(3.0) - 2.3025851 * jax.random.uniform(key_list[4], (LEVELS, SEQ), jnp.float32) ** level_of(key_list[4], (LEVELS, SEQ), ((1, 8),), -0.2, 0.2)), 0.3, 3.0)
    return {"query_rows": query_rows, "key_rows": key_rows, "value_rows": value_rows, "out_grad": out_grad, "level_weights": level_weights}


HIGH = lax.Precision.HIGHEST


def binary_digits(values, top):
    total = jnp.zeros(values.shape, jnp.int32)
    for height in range(top):
        total = total + (values >= (1 << height)).astype(jnp.int32)
    return total


def local_terms(query, keyed, valued, grad_out, fine_weights):
    frames = query.shape[0]
    fine_count = fine_weights.shape[0]
    places = jnp.arange(frames, dtype=jnp.int32)
    target = places[:, None]
    source = places[None, :]
    digits = binary_digits(jnp.bitwise_xor(target, source), fine_count - 1)
    causal = source <= target
    mixing = jnp.zeros((frames, frames), jnp.float32)
    masks = []
    for height in range(fine_count):
        chosen = jnp.logical_and(digits == height, causal)
        masks.append(chosen)
        mixing = mixing + jnp.where(chosen, fine_weights[height][:, None], jnp.float32(0.0))
    scores = jnp.einsum('thd,shd->hts', query, keyed, precision=HIGH)
    backed = jnp.einsum('the,she->hts', grad_out, valued, precision=HIGH)
    back_mixed = backed * mixing[None]
    score_mixed = scores * mixing[None]
    q_grad = jnp.einsum('hts,shd->thd', back_mixed, keyed, precision=HIGH)
    k_grad = jnp.einsum('hts,thd->shd', back_mixed, query, precision=HIGH)
    v_grad = jnp.einsum('hts,the->she', score_mixed, grad_out, precision=HIGH)
    product = jnp.sum(scores * backed, axis=0)
    w_grad = jnp.stack([jnp.sum(jnp.where(chosen, product, jnp.float32(0.0)), axis=1) for chosen in masks])
    return q_grad, k_grad, v_grad, w_grad


def coarse_terms(query, grad_out, states, coarse_weights):
    along = jnp.einsum('the,lhde->lthd', grad_out, states, precision=HIGH)
    q_grad = jnp.einsum('lt,lthd->thd', coarse_weights, along, precision=HIGH)
    w_grad = jnp.einsum('thd,lthd->lt', query, along, precision=HIGH)
    state_grad = jnp.einsum('lt,thd,the->lhde', coarse_weights, query, grad_out, precision=HIGH)
    return q_grad, w_grad, state_grad


def reference(query_rows, key_rows, value_rows, out_grad, level_weights):
    shape = (N_TM, F, HEADS, DK)
    queries = query_rows.reshape(shape)
    keyset = key_rows.reshape(shape)
    valueset = value_rows.reshape(shape)
    grads = out_grad.reshape(shape)
    fine_count = LEV_FR + 1
    blocks_w = level_weights.reshape(LEVELS, N_TM, F).transpose(1, 0, 2)
    states = jnp.einsum('bshd,bshe->bhde', keyset, valueset, precision=HIGH)
    devices = jnp.arange(N_TM, dtype=jnp.int32)
    digits = binary_digits(jnp.bitwise_xor(devices[:, None], devices[None, :]), LEV_TM)
    wanted = jnp.arange(1, LEV_TM + 1, dtype=jnp.int32)
    chosen = jnp.logical_and(digits[:, :, None] == wanted[None, None, :], (devices[None, :] < devices[:, None])[:, :, None])
    tables = chosen.astype(jnp.float32)
    sibling = jnp.einsum('bjl,jhde->blhde', tables, states, precision=HIGH)

    def per_block(items):
        query, keyed, valued, grad_out, weights, block_states = items
        q_grad, k_grad, v_grad, w_fine = local_terms(query, keyed, valued, grad_out, weights[:fine_count])
        q_coarse, w_coarse, state_grad = coarse_terms(query, grad_out, block_states, weights[fine_count:])
        return q_grad + q_coarse, k_grad, v_grad, jnp.concatenate([w_fine, w_coarse], axis=0), state_grad

    q_grad, k_grad, v_grad, w_grad, state_grads = lax.map(per_block, (queries, keyset, valueset, grads, blocks_w, sibling))
    state_back = jnp.einsum('bjl,blhde->jhde', tables, state_grads, precision=HIGH)
    k_grad = k_grad + jnp.einsum('bshe,bhde->bshd', valueset, state_back, precision=HIGH)
    v_grad = v_grad + jnp.einsum('bshd,bhde->bshe', keyset, state_back, precision=HIGH)
    flat = (SEQ, HEADS * DK)
    weight_grad = w_grad.transpose(1, 0, 2).reshape(LEVELS, SEQ)
    return q_grad.reshape(flat), k_grad.reshape(flat), v_grad.reshape(flat), weight_grad
```

```python
import functools

import jax
import jax.numpy as jnp
from jax import lax
from jax.experimental import pallas as pl
from jax.experimental.pallas import tpu as pltpu
from jax.sharding import PartitionSpec as P

DK = 128
C = 128
SUB = 8
NN = (((1,), (0,)), ((), ()))
NT = (((1,), (1,)), ((), ()))
TN = (((0,), (0,)), ((), ()))


def partner(array, axis, stride):
    return lax.ppermute(array, axis, [(i, i ^ 1 << stride) for i in range(lax.axis_size(axis))])


def split(x):
    hi = x.astype(jnp.bfloat16)
    return hi, (x - hi.astype(jnp.float32)).astype(jnp.bfloat16)


def wide(parts):
    return jnp.concatenate(parts, axis=1)


def tall(parts):
    return jnp.concatenate(parts, axis=0)


def dot(a, b, dims):
    return lax.dot_general(a, b, dims, preferred_element_type=jnp.float32)


def halves(x):
    n = x.shape[1] // 2
    return x[:, :n] + x[:, n:]


def nn(a, b):
    right = wide(b)
    return halves(dot(wide(a), tall((right, right)), NN))


def nt(a, b):
    return halves(dot(wide(a), tall((wide((b[0], b[0])), wide((b[1], b[1])))), NT))


def tn(a, b):
    right = wide(b)
    return halves(dot(tall(a), tall((right, right)), TN))


def fold(x):
    return jnp.sum(x.reshape(x.shape[0] // SUB, SUB, x.shape[1]), axis=0)


def level_table():
    s = lax.broadcasted_iota(jnp.int32, (C, C), 0)
    t = lax.broadcasted_iota(jnp.int32, (C, C), 1)
    x = jnp.bitwise_xor(s, t)
    level = jnp.zeros((C, C), jnp.int32)
    for height in range(C.bit_length() - 1):
        level = level + (x >= 1 << height).astype(jnp.int32)
    return jnp.where(s <= t, level, -1)


def state_kernel(first, q_ref, k_ref, v_ref, d_ref, w_ref, s_ref, g_ref):
    frames = q_ref.shape[0]
    vv = wide(split(v_ref[...]))
    kh, kl = split(k_ref[...])
    s_ref[0] = halves(dot(kh, vv, TN) + dot(kl, vv, TN))
    dd = wide(split(d_ref[...]))
    qt = q_ref[...].T
    for level in range(g_ref.shape[0]):
        gh, gl = split(qt * w_ref[first + level : first + level + 1, :])
        g_ref[level, 0] = halves(dot(gh, dd, NN) + dot(gl, dd, NN))


def upper_pairs(chunks):
    heights = chunks.bit_length() - 1
    return [(c, k) for c in range(chunks) for k in range(heights) if c >> k & 1]


def local_kernel(q_ref, k_ref, v_ref, d_ref, w_ref, qg_ref, kg_ref, vg_ref, wg_ref, mt_ref, pr_ref, wc_ref):
    head = pl.program_id(0)
    frames = q_ref.shape[0]
    chunks = frames // C
    heights = chunks.bit_length() - 1
    inner = C.bit_length()
    pairs = upper_pairs(chunks)
    spans = [slice(c * C, (c + 1) * C) for c in range(chunks)]

    @pl.when(head == 0)
    def _():
        table = level_table()
        for c in range(chunks):
            mixing = jnp.zeros((C, C), jnp.float32)
            for level in range(inner):
                mixing = jnp.where(table == level, w_ref[level : level + 1, spans[c]], mixing)
            mt_ref[c] = mixing
        pr_ref[...] = jnp.zeros_like(pr_ref)
        wc_ref[...] = jnp.zeros_like(wc_ref)

    sums = {}
    for c in range(chunks):
        ks = split(k_ref[spans[c], :])
        vs = split(v_ref[spans[c], :])
        if c < chunks - 1:
            sums[c, 0] = tn(ks, vs)
    for k in range(1, heights):
        for b in range(chunks >> k):
            if b << k < chunks - (1 << k):
                sums[b, k] = sums[2 * b, k - 1] + sums[2 * b + 1, k - 1]
    back = {}
    for c in range(chunks):
        q = q_ref[spans[c], :]
        qs, ks = split(q), split(k_ref[spans[c], :])
        vs, ds = split(v_ref[spans[c], :]), split(d_ref[spans[c], :])
        gt = nt(ks, qs)
        et = nt(vs, ds)
        pr_ref[c] += gt * et
        mt = mt_ref[c]
        me, mg = split(mt * et), split(mt * gt)
        kg_ref[spans[c], :] = nn(me, qs)
        vg_ref[spans[c], :] = nn(mg, ds)
        qg = tn(me, ks)
        ups = [k for k in range(heights) if c >> k & 1]
        if ups:
            qt = q.T
            mixed = None
            for k in ups:
                row = w_ref[inner + k : inner + k + 1, spans[c]]
                along = nt(split(sums[(c >> k) - 1, k]), ds)
                wc_ref[pairs.index((c, k))] += fold(qt * along)
                term = row * along
                mixed = term if mixed is None else mixed + term
                grad = nn(split(row * qt), ds)
                key = ((c >> k) - 1, k)
                back[key] = back[key] + grad if key in back else grad
            qg = qg + mixed.T
        qg_ref[spans[c], :] = qg
    for c in range(chunks - 1):
        total = None
        for k in range(heights):
            if not c >> k & 1:
                term = back[c >> k, k]
                total = term if total is None else total + term
        bs = split(total)
        kg_ref[spans[c], :] += nt(split(v_ref[spans[c], :]), bs)
        vg_ref[spans[c], :] += nn(split(k_ref[spans[c], :]), bs)

    @pl.when(head == pl.num_programs(0) - 1)
    def _():
        table = level_table()
        wg_ref[...] = jnp.zeros_like(wg_ref)
        for c in range(chunks):
            product = pr_ref[c]
            for level in range(inner):
                row = jnp.sum(jnp.where(table == level, product, 0.0), axis=0, keepdims=True)
                wg_ref[level : level + 1, spans[c]] = row
        for i, (c, k) in enumerate(pairs):
            wg_ref[inner + k : inner + k + 1, spans[c]] = jnp.sum(wc_ref[i], axis=0, keepdims=True)


def coarse_kernel(first, q_ref, d_ref, w_ref, s_ref, qg_ref, out_ref, wg_ref, wc_ref):
    head = pl.program_id(0)
    frames = q_ref.shape[0]
    levels = s_ref.shape[0]
    states = [split(s_ref[level, 0]) for level in range(levels)]
    left = tall([wide(s) for s in states])

    @pl.when(head == 0)
    def _():
        wc_ref[...] = jnp.zeros_like(wc_ref)

    for c in range(frames // C):
        span = slice(c * C, (c + 1) * C)
        dh, dl = split(d_ref[span, :])
        along = halves(dot(left, tall((wide((dh, dh)), wide((dl, dl)))), NT))
        qt = q_ref[span, :].T
        mixed = None
        for level in range(levels):
            part = along[level * DK : (level + 1) * DK, :]
            wc_ref[level, :, span] += fold(qt * part)
            term = w_ref[first + level : first + level + 1, span] * part
            mixed = term if mixed is None else mixed + term
        out_ref[span, :] = qg_ref[span, :] + mixed.T

    @pl.when(head == pl.num_programs(0) - 1)
    def _():
        wg_ref[...] = jnp.zeros_like(wg_ref)
        for level in range(levels):
            wg_ref[level : level + 1, :] = jnp.sum(wc_ref[level], axis=0, keepdims=True)


def back_kernel(k_ref, v_ref, b_ref, kg_ref, vg_ref, ko_ref, vo_ref):
    bs = split(b_ref[0])
    ko_ref[...] = kg_ref[...] + nt(split(v_ref[...]), bs)
    vo_ref[...] = vg_ref[...] + nn(split(k_ref[...]), bs)


def params():
    return pltpu.CompilerParams(dimension_semantics=("arbitrary",), vmem_limit_bytes=32 * 2**20)


def local(query_rows, key_rows, value_rows, out_grad, level_weights):
    frames, width = query_rows.shape
    heads = width // DK
    levels = level_weights.shape[0]
    fine = frames.bit_length()
    device_levels = levels - fine
    f32 = jnp.float32
    column = pl.BlockSpec((frames, DK), lambda h: (0, h))
    weights = pl.BlockSpec((levels, frames), lambda h: (0, 0))
    state = pl.BlockSpec((1, DK, DK), lambda h: (h, 0, 0))
    stack = pl.BlockSpec((device_levels, 1, DK, DK), lambda h: (0, h, 0, 0))
    big = jax.ShapeDtypeStruct((frames, width), f32)
    fine_rows = -(-fine // SUB) * SUB
    coarse_rows = -(-device_levels // SUB) * SUB
    chunks = frames // C

    states, state_grads = pl.pallas_call(
        functools.partial(state_kernel, fine),
        grid=(heads,),
        in_specs=[column] * 4 + [weights],
        out_specs=[state, stack],
        out_shape=[
            jax.ShapeDtypeStruct((heads, DK, DK), f32),
            jax.ShapeDtypeStruct((device_levels, heads, DK, DK), f32),
        ],
        compiler_params=params(),
        name="states",
    )(query_rows, key_rows, value_rows, out_grad, level_weights)

    q_local, k_local, v_local, w_fine = pl.pallas_call(
        local_kernel,
        grid=(heads,),
        in_specs=[column] * 4 + [weights],
        out_specs=[column] * 3 + [pl.BlockSpec((fine_rows, frames), lambda h: (0, 0))],
        out_shape=[big] * 3 + [jax.ShapeDtypeStruct((fine_rows, frames), f32)],
        scratch_shapes=[
            pltpu.VMEM((chunks, C, C), f32),
            pltpu.VMEM((chunks, C, C), f32),
            pltpu.VMEM((max(1, len(upper_pairs(chunks))), SUB, C), f32),
        ],
        compiler_params=params(),
        name="inside",
    )(query_rows, key_rows, value_rows, out_grad, level_weights)

    device = lax.axis_index("tm")
    block = states
    found = []
    for height in range(device_levels):
        other = partner(block, "tm", height)
        upper = jnp.bitwise_and(jnp.right_shift(device, height), 1) == 1
        found.append(jnp.where(upper, other, jnp.float32(0.0)))
        block = block + other
    sibling = jnp.stack(found)
    upper = jnp.bitwise_and(jnp.right_shift(device, jnp.arange(device_levels)), 1) == 1
    carried = state_grads
    state_back = jnp.zeros_like(states)
    for height in range(device_levels):
        other = partner(carried[height:], "tm", height)
        lower = jnp.bitwise_and(jnp.right_shift(device, height), 1) == 0
        state_back = state_back + jnp.where(lower, other[0], jnp.float32(0.0))
        carried = jnp.concatenate([carried[:height], carried[height:] + other], axis=0)

    q_total, w_coarse = pl.pallas_call(
        functools.partial(coarse_kernel, fine),
        grid=(heads,),
        in_specs=[column] * 2 + [weights, stack, column],
        out_specs=[column, pl.BlockSpec((coarse_rows, frames), lambda h: (0, 0))],
        out_shape=[big, jax.ShapeDtypeStruct((coarse_rows, frames), f32)],
        scratch_shapes=[pltpu.VMEM((device_levels, SUB, frames), f32)],
        input_output_aliases={4: 0},
        compiler_params=params(),
        name="coarse",
    )(query_rows, out_grad, level_weights, sibling, q_local)

    weight_terms = jnp.concatenate([w_fine[:fine], w_coarse[:device_levels]], axis=0)
    weight_grad = lax.psum(weight_terms, "head")

    k_total, v_total = pl.pallas_call(
        back_kernel,
        grid=(heads,),
        in_specs=[column] * 2 + [state, column, column],
        out_specs=[column] * 2,
        out_shape=[big] * 2,
        input_output_aliases={3: 0, 4: 1},
        compiler_params=params(),
        name="back",
    )(key_rows, value_rows, state_back, k_local, v_local)
    return (q_total, k_total, v_total, weight_grad)


def solution(mesh):
    in_specs = (P("tm", "head"), P("tm", "head"), P("tm", "head"), P("tm", "head"), P(None, "tm"))
    out_specs = (P("tm", "head"), P("tm", "head"), P("tm", "head"), P(None, "tm"))
    return jax.shard_map(local, mesh=mesh, in_specs=in_specs, out_specs=out_specs, check_vma=False)
```

```python
import functools

import jax
import jax.numpy as jnp
from jax import lax
from jax.experimental import pallas as pl
from jax.experimental.pallas import tpu as pltpu
from jax.sharding import PartitionSpec as P


DK = 128
C = 128
SUB = 8
NN = (((1,), (0,)), ((), ()))
NT = (((1,), (1,)), ((), ()))
TN = (((0,), (0,)), ((), ()))


def partner(array, axis, stride):
    return lax.ppermute(array, axis, [(i, i ^ 1 << stride) for i in range(lax.axis_size(axis))])


def split(x):
    hi = x.astype(jnp.bfloat16)
    return hi, (x - hi.astype(jnp.float32)).astype(jnp.bfloat16)


def wide(parts):
    return jnp.concatenate(parts, axis=1)


def tall(parts):
    return jnp.concatenate(parts, axis=0)


def dot(a, b, dims):
    return lax.dot_general(a, b, dims, preferred_element_type=jnp.float32)


def halves(x):
    n = x.shape[1] // 2
    return x[:, :n] + x[:, n:]


def nn(a, b):
    right = wide(b)
    return halves(dot(wide(a), tall((right, right)), NN))


def nt(a, b):
    return halves(dot(wide(a), tall((wide((b[0], b[0])), wide((b[1], b[1])))), NT))


def tn(a, b):
    right = wide(b)
    return halves(dot(tall(a), tall((right, right)), TN))


def fold(x):
    return jnp.sum(x.reshape(x.shape[0] // SUB, SUB, x.shape[1]), axis=0)


def level_table():
    s = lax.broadcasted_iota(jnp.int32, (C, C), 0)
    t = lax.broadcasted_iota(jnp.int32, (C, C), 1)
    x = jnp.bitwise_xor(s, t)
    level = jnp.zeros((C, C), jnp.int32)
    for height in range(C.bit_length() - 1):
        level = level + (x >= 1 << height).astype(jnp.int32)
    return jnp.where(s <= t, level, -1)


def head_order(i, own, heads):
    return (i + (1 - own) * (heads // 2)) % heads


def state_kernel(first, bits_ref, q_ref, k_ref, v_ref, d_ref, w_ref, near_ref, send_ref, keep_ref, mix_ref):
    step = pl.program_id(0)
    half = pl.num_programs(0) // 2
    levels = send_ref.shape[0] + 1
    chunks, inner = mix_ref.shape[0], C.bit_length()

    @pl.when(step == 0)
    def _():
        table = level_table()
        for c in range(chunks):
            mixing = jnp.zeros((C, C), jnp.float32)
            for level in range(inner):
                mixing = jnp.where(table == level, w_ref[level : level + 1, c * C : (c + 1) * C], mixing)
            mix_ref[c] = mixing

    vv = wide(split(v_ref[...]))
    kh, kl = split(k_ref[...])
    state = halves(dot(kh, vv, TN) + dot(kl, vv, TN))
    dd = wide(split(d_ref[...]))
    qt = q_ref[...].T
    for level in range(levels):
        gh, gl = split(qt * w_ref[first + level : first + level + 1, :])
        grad = halves(dot(gh, dd, NN) + dot(gl, dd, NN))
        moved = jnp.where(bits_ref[level] == 1, grad, state)
        if level == 0:
            near_ref[0] = moved
        else:

            @pl.when(step < half)
            def _(level=level, moved=moved):
                send_ref[level - 1, 0] = moved

            @pl.when(step >= half)
            def _(level=level, moved=moved):
                keep_ref[level - 1, 0] = moved


def upper_pairs(chunks):
    heights = chunks.bit_length() - 1
    return [(c, k) for c in range(chunks) for k in range(heights) if c >> k & 1]


def local_kernel(start, last, *refs):
    q_ref, k_ref, v_ref, d_ref, w_ref, mix_ref = refs[:6]
    if start:
        qg_ref, kg_ref, vg_ref, pr_ref, wc_ref = refs[6:11]
    else:
        old_pr, old_wc = refs[9:11]
        qg_ref, kg_ref, vg_ref, pr_ref, wc_ref = refs[11:16]
    head = pl.program_id(0)
    frames = q_ref.shape[0]
    chunks = frames // C
    heights = chunks.bit_length() - 1
    inner = C.bit_length()
    pairs = upper_pairs(chunks)
    spans = [slice(c * C, (c + 1) * C) for c in range(chunks)]

    @pl.when(head == 0)
    def _():
        pr_ref[...] = jnp.zeros_like(pr_ref) if start else old_pr[...]
        wc_ref[...] = jnp.zeros_like(wc_ref) if start else old_wc[...]

    sums = {}
    for c in range(chunks):
        ks = split(k_ref[spans[c], :])
        vs = split(v_ref[spans[c], :])
        if c < chunks - 1:
            sums[c, 0] = tn(ks, vs)
    for k in range(1, heights):
        for b in range(chunks >> k):
            if b << k < chunks - (1 << k):
                sums[b, k] = sums[2 * b, k - 1] + sums[2 * b + 1, k - 1]
    back = {}
    for c in range(chunks):
        q = q_ref[spans[c], :]
        qs, ks = split(q), split(k_ref[spans[c], :])
        vs, ds = split(v_ref[spans[c], :]), split(d_ref[spans[c], :])
        gt = nt(ks, qs)
        et = nt(vs, ds)
        pr_ref[c] += gt * et
        mt = mix_ref[c]
        me, mg = split(mt * et), split(mt * gt)
        kg_ref[spans[c], :] = nn(me, qs)
        vg_ref[spans[c], :] = nn(mg, ds)
        qg = tn(me, ks)
        ups = [k for k in range(heights) if c >> k & 1]
        if ups:
            qt = q.T
            mixed = None
            for k in ups:
                row = w_ref[inner + k : inner + k + 1, spans[c]]
                along = nt(split(sums[(c >> k) - 1, k]), ds)
                wc_ref[pairs.index((c, k))] += fold(qt * along)
                term = row * along
                mixed = term if mixed is None else mixed + term
                grad = nn(split(row * qt), ds)
                key = ((c >> k) - 1, k)
                back[key] = back[key] + grad if key in back else grad
            qg = qg + mixed.T
        qg_ref[spans[c], :] = qg
    for c in range(chunks - 1):
        total = None
        for k in range(heights):
            if not c >> k & 1:
                term = back[c >> k, k]
                total = term if total is None else total + term
        bs = split(total)
        kg_ref[spans[c], :] += nt(split(v_ref[spans[c], :]), bs)
        vg_ref[spans[c], :] += nn(split(k_ref[spans[c], :]), bs)

    if last:
        wg_ref = refs[-1]

        @pl.when(head == pl.num_programs(0) - 1)
        def _():
            table = level_table()
            wg_ref[...] = jnp.zeros_like(wg_ref)
            for c in range(chunks):
                product = pr_ref[c]
                for level in range(inner):
                    row = jnp.sum(jnp.where(table == level, product, 0.0), axis=0, keepdims=True)
                    wg_ref[level : level + 1, spans[c]] = row
            for i, (c, k) in enumerate(pairs):
                wg_ref[inner + k : inner + k + 1, spans[c]] = jnp.sum(wc_ref[i], axis=0, keepdims=True)


def received(refs, levels):
    step = pl.program_id(0)
    half = pl.num_programs(0) // 2
    found = [refs[0][0]]
    for level in range(1, levels):
        found.append(jnp.where(step < half, refs[2 * level - 1][0], refs[2 * level][0]))
    return found


def coarse_kernel(first, levels, bits_ref, *refs):
    q_ref, d_ref, w_ref = refs[:3]
    arrived = refs[3 : 2 + 2 * levels]
    qg_ref, out_ref, wg_ref, wc_ref = refs[2 + 2 * levels :]
    step = pl.program_id(0)
    frames = q_ref.shape[0]
    states = []
    for level, state in enumerate(received(arrived, levels)):
        states.append(split(jnp.where(bits_ref[level] == 1, state, 0.0)))
    left = tall([wide(s) for s in states])

    @pl.when(step == 0)
    def _():
        wc_ref[...] = jnp.zeros_like(wc_ref)

    for c in range(frames // C):
        span = slice(c * C, (c + 1) * C)
        dh, dl = split(d_ref[span, :])
        along = halves(dot(left, tall((wide((dh, dh)), wide((dl, dl)))), NT))
        qt = q_ref[span, :].T
        mixed = None
        for level in range(levels):
            part = along[level * DK : (level + 1) * DK, :]
            wc_ref[level, :, span] += fold(qt * part)
            term = w_ref[first + level : first + level + 1, span] * part
            mixed = term if mixed is None else mixed + term
        out_ref[span, :] = qg_ref[span, :] + mixed.T

    @pl.when(step == pl.num_programs(0) - 1)
    def _():
        wg_ref[...] = jnp.zeros_like(wg_ref)
        for level in range(levels):
            wg_ref[level : level + 1, :] = jnp.sum(wc_ref[level], axis=0, keepdims=True)


def back_kernel(levels, bits_ref, *refs):
    k_ref, v_ref = refs[:2]
    arrived = refs[2 : 1 + 2 * levels]
    kg_ref, vg_ref, ko_ref, vo_ref = refs[1 + 2 * levels :]
    total = None
    for level, state in enumerate(received(arrived, levels)):
        term = jnp.where(bits_ref[level] == 0, state, 0.0)
        total = term if total is None else total + term
    bs = split(total)
    ko_ref[...] = kg_ref[...] + nt(split(v_ref[...]), bs)
    vo_ref[...] = vg_ref[...] + nn(split(k_ref[...]), bs)


def params(mib):
    return pltpu.CompilerParams(dimension_semantics=("arbitrary",), vmem_limit_bytes=mib * 2**20)


def cost(flops, size):
    return pl.CostEstimate(flops=flops, bytes_accessed=size, transcendentals=0)


def body(query_rows, key_rows, value_rows, out_grad, level_weights):
    frames, width = query_rows.shape
    heads = width // DK
    half = heads // 2
    levels = level_weights.shape[0]
    fine = frames.bit_length()
    device_levels = levels - fine
    far = device_levels - 1
    f32 = jnp.float32
    big = jax.ShapeDtypeStruct((frames, width), f32)
    fine_rows = -(-fine // SUB) * SUB
    coarse_rows = -(-device_levels // SUB) * SUB
    chunks = frames // C
    pairs = max(1, len(upper_pairs(chunks)))
    block = frames * width * 4
    device = lax.axis_index("tm")
    bits = jnp.bitwise_and(jnp.right_shift(device, jnp.arange(device_levels)), 1).astype(jnp.int32)

    def whole(shape):
        return pl.BlockSpec(shape, lambda i, *s: (0,) * len(shape))

    ordered = pl.BlockSpec((frames, DK), lambda i, b: (0, head_order(i, b[0], heads)))
    first_half = lambda i: jnp.minimum(i, half - 1)
    second_half = lambda i: jnp.maximum(i - half, 0)

    near, send, keep, mix = pl.pallas_call(
        functools.partial(state_kernel, fine),
        grid_spec=pltpu.PrefetchScalarGridSpec(
            num_scalar_prefetch=1,
            grid=(heads,),
            in_specs=[ordered] * 4 + [whole((levels, frames))],
            out_specs=[
                pl.BlockSpec((1, DK, DK), lambda i, b: (head_order(i, b[0], heads), 0, 0)),
                pl.BlockSpec((far, 1, DK, DK), lambda i, b: (0, first_half(i), 0, 0)),
                pl.BlockSpec((far, 1, DK, DK), lambda i, b: (0, second_half(i), 0, 0)),
                whole((chunks, C, C)),
            ],
        ),
        out_shape=[
            jax.ShapeDtypeStruct((heads, DK, DK), f32),
            jax.ShapeDtypeStruct((far, half, DK, DK), f32),
            jax.ShapeDtypeStruct((far, half, DK, DK), f32),
            jax.ShapeDtypeStruct((chunks, C, C), f32),
        ],
        compiler_params=params(58),
        cost_estimate=cost(10**9, 4 * block),
        name="states",
    )(bits, query_rows, key_rows, value_rows, out_grad, level_weights)

    local = None
    for piece in range(heads):
        start, last = piece == 0, piece == heads - 1
        column = pl.BlockSpec((frames, DK), lambda i, piece=piece: (0, piece + i))
        anywhere = pl.BlockSpec(memory_space=pl.ANY)
        carry = [whole((chunks, C, C)), whole((pairs, SUB, C))]
        shapes = [big] * 3 + [jax.ShapeDtypeStruct((chunks, C, C), f32), jax.ShapeDtypeStruct((pairs, SUB, C), f32)]
        local = pl.pallas_call(
            functools.partial(local_kernel, start, last),
            grid=(1,),
            in_specs=[column] * 4
            + [whole((levels, frames)), whole((chunks, C, C))]
            + ([] if start else [anywhere] * 3 + carry),
            out_specs=[column] * 3 + carry + ([whole((fine_rows, frames))] if last else []),
            out_shape=shapes + ([jax.ShapeDtypeStruct((fine_rows, frames), f32)] if last else []),
            input_output_aliases={} if start else {6 + i: i for i in range(5)},
            compiler_params=params(58),
            cost_estimate=cost(10**9, 7 * block // heads),
        )(query_rows, key_rows, value_rows, out_grad, level_weights, mix, *(local or []))
    q_local, k_local, v_local, _, _, w_fine = local

    arrived = []
    carried = keep + partner(send, "tm", 0)
    for height in range(1, device_levels):
        other = partner(carried, "tm", height)
        arrived.append(other[0])
        carried = carried[1:] + other[1:]
    states = [partner(near, "tm", 0)]
    for height in range(far):
        states += [partner(arrived[height], "tm", 0), arrived[height]]

    state_specs = [pl.BlockSpec((1, DK, DK), lambda i, b: (head_order(i, b[0], heads), 0, 0))]
    for _ in range(far):
        state_specs.append(pl.BlockSpec((1, DK, DK), lambda i, b: (first_half(i), 0, 0)))
        state_specs.append(pl.BlockSpec((1, DK, DK), lambda i, b: (second_half(i), 0, 0)))

    q_total, w_coarse = pl.pallas_call(
        functools.partial(coarse_kernel, fine, device_levels),
        grid_spec=pltpu.PrefetchScalarGridSpec(
            num_scalar_prefetch=1,
            grid=(heads,),
            in_specs=[ordered] * 2 + [whole((levels, frames))] + state_specs + [ordered],
            out_specs=[ordered, whole((coarse_rows, frames))],
            scratch_shapes=[pltpu.VMEM((device_levels, SUB, frames), f32)],
        ),
        out_shape=[big, jax.ShapeDtypeStruct((coarse_rows, frames), f32)],
        input_output_aliases={4 + len(state_specs): 0},
        compiler_params=params(58),
        cost_estimate=cost(10**9, 4 * block),
        name="coarse",
    )(bits, query_rows, out_grad, level_weights, *states, q_local)

    weight_grad = jnp.concatenate([w_fine[:fine], w_coarse[:device_levels]], axis=0)
    for height in range(lax.axis_size("head").bit_length() - 1):
        weight_grad = weight_grad + partner(weight_grad, "head", height)

    k_total, v_total = pl.pallas_call(
        functools.partial(back_kernel, device_levels),
        grid_spec=pltpu.PrefetchScalarGridSpec(
            num_scalar_prefetch=1,
            grid=(heads,),
            in_specs=[ordered] * 2 + state_specs + [ordered] * 2,
            out_specs=[ordered] * 2,
        ),
        out_shape=[big] * 2,
        input_output_aliases={3 + len(state_specs): 0, 4 + len(state_specs): 1},
        compiler_params=params(58),
        cost_estimate=cost(10**9, 6 * block),
        name="back",
    )(bits, key_rows, value_rows, *states, k_local, v_local)
    return (q_total, k_total, v_total, weight_grad)


def solution(mesh):
    in_specs = (P("tm", "head"), P("tm", "head"), P("tm", "head"), P("tm", "head"), P(None, "tm"))
    out_specs = (P("tm", "head"), P("tm", "head"), P("tm", "head"), P(None, "tm"))
    return jax.shard_map(body, mesh=mesh, in_specs=in_specs, out_specs=out_specs, check_vma=False)
```

```python
import functools

import jax
import jax.numpy as jnp
from jax import lax
from jax.experimental import pallas as pl
from jax.experimental.pallas import tpu as pltpu
from jax.sharding import PartitionSpec as P


DK = 128
C = 128
B = 256
SUB = 8
NN = (((1,), (0,)), ((), ()))
NT = (((1,), (1,)), ((), ()))
TN = (((0,), (0,)), ((), ()))


def partner(array, axis, stride):
    return lax.ppermute(array, axis, [(i, i ^ 1 << stride) for i in range(lax.axis_size(axis))])


def split(x):
    hi = x.astype(jnp.bfloat16)
    return hi, (x - hi.astype(jnp.float32)).astype(jnp.bfloat16)


def wide(parts):
    return jnp.concatenate(parts, axis=1)


def tall(parts):
    return jnp.concatenate(parts, axis=0)


def dot(a, b, dims):
    return lax.dot_general(a, b, dims, preferred_element_type=jnp.float32)


def halves(x):
    n = x.shape[1] // 2
    return x[:, :n] + x[:, n:]


def nn(a, b):
    right = wide(b)
    return halves(dot(wide(a), tall((right, right)), NN))


def nt(a, b):
    return halves(dot(wide(a), tall((wide((b[0], b[0])), wide((b[1], b[1])))), NT))


def tn(a, b):
    right = wide(b)
    return halves(dot(tall(a), tall((right, right)), TN))


def fold(x):
    return jnp.sum(x.reshape(x.shape[0] // SUB, SUB, x.shape[1]), axis=0)


def level_table():
    s = lax.broadcasted_iota(jnp.int32, (C, C), 0)
    t = lax.broadcasted_iota(jnp.int32, (C, C), 1)
    x = jnp.bitwise_xor(s, t)
    level = jnp.zeros((C, C), jnp.int32)
    for height in range(C.bit_length() - 1):
        level = level + (x >= 1 << height).astype(jnp.int32)
    return jnp.where(s <= t, level, -1)


def head_order(i, own, heads):
    return (i + (1 - own) * (heads // 2)) % heads


def state_kernel(first, bits_ref, q_ref, k_ref, v_ref, d_ref, w_ref, near_ref, send_ref, keep_ref, mix_ref, left_ref, right_ref, turned_ref, sum_ref):
    step = pl.program_id(0)
    heads = pl.num_programs(0)
    half = heads // 2
    head = head_order(step, bits_ref[0], heads)
    levels = send_ref.shape[0] + 1
    frames = q_ref.shape[0]
    chunks, inner = mix_ref.shape[0], C.bit_length()

    @pl.when(step == 0)
    def _():
        table = level_table()
        for c in range(chunks):
            mixing = jnp.zeros((C, C), jnp.float32)
            for level in range(inner):
                mixing = jnp.where(table == level, w_ref[level : level + 1, c * C : (c + 1) * C], mixing)
            mix_ref[c] = mixing

    for b in range(frames // B):
        span = slice(b * B, (b + 1) * B)
        k, q = k_ref[span, :], q_ref[span, :]
        left_ref[0, head, span, :] = wide(split(k))
        left_ref[1, head, span, :] = wide(split(q))
        right_ref[0, head, span, :] = wide(split(v_ref[span, :]))
        right_ref[1, head, span, :] = wide(split(d_ref[span, :]))
        turned_ref[0, head, :, span] = k.T
        turned_ref[1, head, :, span] = q.T
        for level in range(levels):
            bit = bits_ref[level]
            row = jnp.where(bit == 1, w_ref[first + level : first + level + 1, span], 1.0)
            grown = wide(split(row * turned_ref[bit, head, :, span]))
            right = right_ref[bit, head, span, :]
            term = dot(grown, tall((right, right)), NN)
            sum_ref[level] = term if b == 0 else sum_ref[level] + term
    near_ref[0] = halves(sum_ref[0])

    @pl.when(step < half)
    def _():
        for level in range(1, levels):
            send_ref[level - 1, 0] = halves(sum_ref[level])

    @pl.when(step >= half)
    def _():
        for level in range(1, levels):
            keep_ref[level - 1, 0] = halves(sum_ref[level])


def upper_pairs(chunks):
    heights = chunks.bit_length() - 1
    return [(c, k) for c in range(chunks) for k in range(heights) if c >> k & 1]


def parts(ref, *at):
    x = ref[at]
    return x[:, :DK], x[:, DK:]


def local_kernel(head, last, left_ref, right_ref, turned_ref, w_ref, mix_ref, *refs):
    if head:
        refs = refs[5:]
    qg_ref, kg_ref, vg_ref, pr_ref, wc_ref = refs[:5]
    frames = left_ref.shape[2]
    chunks = frames // C
    heights = chunks.bit_length() - 1
    inner = C.bit_length()
    pairs = upper_pairs(chunks)
    spans = [slice(c * C, (c + 1) * C) for c in range(chunks)]
    lanes = slice(head * DK, (head + 1) * DK)

    def add(ref, at, value):
        ref[at] = ref[at] + value if head else value

    sums = {}
    for c in range(chunks - 1):
        sums[c, 0] = tn(parts(left_ref, 0, head, spans[c]), parts(right_ref, 0, head, spans[c]))
    for k in range(1, heights):
        for b in range(chunks >> k):
            if b << k < chunks - (1 << k):
                sums[b, k] = sums[2 * b, k - 1] + sums[2 * b + 1, k - 1]

    def scores(c):
        ks, qs = parts(left_ref, 0, head, spans[c]), parts(left_ref, 1, head, spans[c])
        vs, ds = parts(right_ref, 0, head, spans[c]), parts(right_ref, 1, head, spans[c])
        gt = nt(ks, qs)
        et = nt(vs, ds)
        add(pr_ref, c, gt * et)
        mt = mix_ref[c]
        return split(mt * et), split(mt * gt)

    back = {}

    def gradients(c, me, mg):
        ks, qs = parts(left_ref, 0, head, spans[c]), parts(left_ref, 1, head, spans[c])
        vs, ds = parts(right_ref, 0, head, spans[c]), parts(right_ref, 1, head, spans[c])
        kg, vg, qg = nn(me, qs), nn(mg, ds), tn(me, ks)
        if c < chunks - 1:
            total = None
            for k in range(heights):
                if not c >> k & 1:
                    term = back[c >> k, k]
                    total = term if total is None else total + term
            bs = split(total)
            kg = kg + nt(vs, bs)
            vg = vg + nn(ks, bs)
        kg_ref[spans[c], lanes] = kg
        vg_ref[spans[c], lanes] = vg
        ups = [k for k in range(heights) if c >> k & 1]
        if ups:
            qt = turned_ref[1, head, :, spans[c]]
            mixed = None
            for k in ups:
                row = w_ref[inner + k : inner + k + 1, spans[c]]
                along = nt(split(sums[(c >> k) - 1, k]), ds)
                add(wc_ref, pairs.index((c, k)), fold(qt * along))
                term = row * along
                mixed = term if mixed is None else mixed + term
                grad = nn(split(row * qt), ds)
                key = ((c >> k) - 1, k)
                back[key] = back[key] + grad if key in back else grad
            qg = qg + mixed.T
        qg_ref[spans[c], lanes] = qg

    waiting = None
    for c in reversed(range(chunks)):
        now = scores(c)
        if waiting is not None:
            gradients(c + 1, *waiting)
        waiting = now
    gradients(0, *waiting)

    if last:
        wg_ref = refs[-1]
        table = level_table()
        wg_ref[...] = jnp.zeros_like(wg_ref)
        for c in range(chunks):
            product = pr_ref[c]
            for level in range(inner):
                row = jnp.sum(jnp.where(table == level, product, 0.0), axis=0, keepdims=True)
                wg_ref[level : level + 1, spans[c]] = row
        for i, (c, k) in enumerate(pairs):
            wg_ref[inner + k : inner + k + 1, spans[c]] = jnp.sum(wc_ref[i], axis=0, keepdims=True)


def received(refs, levels):
    step = pl.program_id(0)
    half = pl.num_programs(0) // 2
    found = [refs[0][0]]
    for level in range(1, levels):
        found.append(jnp.where(step < half, refs[2 * level - 1][0], refs[2 * level][0]))
    return found


def coarse_kernel(first, levels, bits_ref, right_ref, turned_ref, w_ref, qg_ref, *refs):
    arrived = refs[: 2 * levels - 1]
    out_ref, wg_ref, wc_ref = refs[2 * levels - 1 :]
    step = pl.program_id(0)
    heads = pl.num_programs(0)
    head = head_order(step, bits_ref[0], heads)
    frames = qg_ref.shape[0]
    lanes = pl.ds(pl.multiple_of(head * DK, DK), DK)
    states = []
    for level, state in enumerate(received(arrived, levels)):
        states.append(split(jnp.where(bits_ref[level] == 1, state, 0.0)))
    left = tall([wide(s) for s in states])

    @pl.when(step == 0)
    def _():
        wc_ref[...] = jnp.zeros_like(wc_ref)

    for c in range(frames // C):
        span = slice(c * C, (c + 1) * C)
        dh, dl = parts(right_ref, 1, head, span)
        along = halves(dot(left, tall((wide((dh, dh)), wide((dl, dl)))), NT))
        qt = turned_ref[1, head, :, span]
        mixed = None
        for level in range(levels):
            part = along[level * DK : (level + 1) * DK, :]
            wc_ref[level, :, span] += fold(qt * part)
            term = w_ref[first + level : first + level + 1, span] * part
            mixed = term if mixed is None else mixed + term
        out_ref[span, :] = qg_ref[span, lanes] + mixed.T

    @pl.when(step == heads - 1)
    def _():
        wg_ref[...] = jnp.zeros_like(wg_ref)
        for level in range(levels):
            wg_ref[level : level + 1, :] = jnp.sum(wc_ref[level], axis=0, keepdims=True)


def back_kernel(levels, bits_ref, left_ref, right_ref, kg_ref, vg_ref, *refs):
    arrived = refs[: 2 * levels - 1]
    ko_ref, vo_ref = refs[2 * levels - 1 :]
    head = head_order(pl.program_id(0), bits_ref[0], pl.num_programs(0))
    lanes = pl.ds(pl.multiple_of(head * DK, DK), DK)
    total = None
    for level, state in enumerate(received(arrived, levels)):
        term = jnp.where(bits_ref[level] == 0, state, 0.0)
        total = term if total is None else total + term
    bs = split(total)
    for b in range(kg_ref.shape[0] // B):
        span = slice(b * B, (b + 1) * B)
        ko_ref[span, :] = kg_ref[span, lanes] + nt(parts(right_ref, 0, head, span), bs)
        vo_ref[span, :] = vg_ref[span, lanes] + nn(parts(left_ref, 0, head, span), bs)


def params(mib):
    return pltpu.CompilerParams(dimension_semantics=("arbitrary",), vmem_limit_bytes=mib * 2**20)


def cost(flops, size):
    return pl.CostEstimate(flops=flops, bytes_accessed=size, transcendentals=0)


def body(query_rows, key_rows, value_rows, out_grad, level_weights):
    frames, width = query_rows.shape
    heads = width // DK
    half = heads // 2
    levels = level_weights.shape[0]
    fine = frames.bit_length()
    device_levels = levels - fine
    far = device_levels - 1
    f32, bf16 = jnp.float32, jnp.bfloat16
    big = jax.ShapeDtypeStruct((frames, width), f32)
    fine_rows = -(-fine // SUB) * SUB
    coarse_rows = -(-device_levels // SUB) * SUB
    chunks = frames // C
    pairs = max(1, len(upper_pairs(chunks)))
    block = frames * width * 4
    device = lax.axis_index("tm")
    bits = jnp.bitwise_and(jnp.right_shift(device, jnp.arange(device_levels)), 1).astype(jnp.int32)
    inputs = [pltpu.with_memory_space_constraint(x, pltpu.HBM) for x in (query_rows, key_rows, value_rows, out_grad)]

    def whole(shape):
        return pl.BlockSpec(shape, lambda i, *s: (0,) * len(shape))

    here = pl.BlockSpec(memory_space=pltpu.VMEM)
    ordered = pl.BlockSpec((frames, DK), lambda i, b: (0, head_order(i, b[0], heads)))
    first_half = lambda i: jnp.minimum(i, half - 1)
    second_half = lambda i: jnp.maximum(i - half, 0)

    near, send, keep, mix, left, right, turned = pl.pallas_call(
        functools.partial(state_kernel, fine),
        grid_spec=pltpu.PrefetchScalarGridSpec(
            num_scalar_prefetch=1,
            grid=(heads,),
            in_specs=[ordered] * 4 + [whole((levels, frames))],
            out_specs=[
                pl.BlockSpec((1, DK, DK), lambda i, b: (head_order(i, b[0], heads), 0, 0)),
                pl.BlockSpec((far, 1, DK, DK), lambda i, b: (0, first_half(i), 0, 0)),
                pl.BlockSpec((far, 1, DK, DK), lambda i, b: (0, second_half(i), 0, 0)),
                here,
                here,
                here,
                here,
            ],
            scratch_shapes=[pltpu.VMEM((device_levels, DK, 2 * DK), f32)],
        ),
        out_shape=[
            jax.ShapeDtypeStruct((heads, DK, DK), f32),
            jax.ShapeDtypeStruct((far, half, DK, DK), f32),
            jax.ShapeDtypeStruct((far, half, DK, DK), f32),
            pltpu.VMEM((chunks, C, C), f32),
            pltpu.VMEM((2, heads, frames, 2 * DK), bf16),
            pltpu.VMEM((2, heads, frames, 2 * DK), bf16),
            pltpu.VMEM((2, heads, DK, frames), f32),
        ],
        compiler_params=params(16),
        cost_estimate=cost(10**9, 4 * block),
        name="states",
    )(bits, *inputs, level_weights)

    inner = None
    for head in range(heads):
        last = head == heads - 1
        shapes = [pltpu.VMEM((frames, width), f32)] * 3
        shapes += [pltpu.VMEM((chunks, C, C), f32), pltpu.VMEM((pairs, SUB, C), f32)]
        inner = pl.pallas_call(
            functools.partial(local_kernel, head, last),
            in_specs=[here] * (10 if head else 5),
            out_specs=[here] * (6 if last else 5),
            out_shape=shapes + ([jax.ShapeDtypeStruct((fine_rows, frames), f32)] if last else []),
            input_output_aliases={5 + i: i for i in range(5)} if head else {},
            compiler_params=pltpu.CompilerParams(vmem_limit_bytes=16 * 2**20),
            cost_estimate=cost(10**9, 7 * block // heads),
        )(left, right, turned, level_weights, mix, *(inner or []))
    q_local, k_local, v_local, _, _, w_fine = inner

    arrived = []
    carried = keep + partner(send, "tm", 0)
    for height in range(1, device_levels):
        other = partner(carried, "tm", height)
        arrived.append(other[0])
        carried = carried[1:] + other[1:]
    states = [partner(near, "tm", 0)]
    for height in range(far):
        states += [partner(arrived[height], "tm", 0), arrived[height]]

    state_specs = [pl.BlockSpec((1, DK, DK), lambda i, b: (head_order(i, b[0], heads), 0, 0))]
    for _ in range(far):
        state_specs.append(pl.BlockSpec((1, DK, DK), lambda i, b: (first_half(i), 0, 0)))
        state_specs.append(pl.BlockSpec((1, DK, DK), lambda i, b: (second_half(i), 0, 0)))

    q_total, w_coarse = pl.pallas_call(
        functools.partial(coarse_kernel, fine, device_levels),
        grid_spec=pltpu.PrefetchScalarGridSpec(
            num_scalar_prefetch=1,
            grid=(heads,),
            in_specs=[here] * 4 + state_specs,
            out_specs=[ordered, whole((coarse_rows, frames))],
            scratch_shapes=[pltpu.VMEM((device_levels, SUB, frames), f32)],
        ),
        out_shape=[big, jax.ShapeDtypeStruct((coarse_rows, frames), f32)],
        compiler_params=params(16),
        cost_estimate=cost(10**9, 4 * block),
        name="coarse",
    )(bits, right, turned, level_weights, q_local, *states)

    weight_grad = jnp.concatenate([w_fine[:fine], w_coarse[:device_levels]], axis=0)
    for height in range(lax.axis_size("head").bit_length() - 1):
        weight_grad = weight_grad + partner(weight_grad, "head", height)

    k_total, v_total = pl.pallas_call(
        functools.partial(back_kernel, device_levels),
        grid_spec=pltpu.PrefetchScalarGridSpec(
            num_scalar_prefetch=1,
            grid=(heads,),
            in_specs=[here] * 4 + state_specs,
            out_specs=[ordered] * 2,
        ),
        out_shape=[big] * 2,
        compiler_params=params(16),
        cost_estimate=cost(10**9, 6 * block),
        name="back",
    )(bits, left, right, k_local, v_local, *states)
    return (q_total, k_total, v_total, weight_grad)


def solution(mesh):
    in_specs = (P("tm", "head"), P("tm", "head"), P("tm", "head"), P("tm", "head"), P(None, "tm"))
    out_specs = (P("tm", "head"), P("tm", "head"), P("tm", "head"), P(None, "tm"))
    return jax.shard_map(body, mesh=mesh, in_specs=in_specs, out_specs=out_specs, check_vma=False)
```

```python
import functools

import jax
import jax.numpy as jnp
from jax import lax
from jax.experimental import pallas as pl
from jax.experimental.pallas import tpu as pltpu
from jax.sharding import PartitionSpec as P


DK = 128
C = 128
B = 256
SUB = 8
NN = (((1,), (0,)), ((), ()))
NT = (((1,), (1,)), ((), ()))
TN = (((0,), (0,)), ((), ()))


def partner(array, axis, stride):
    return lax.ppermute(array, axis, [(i, i ^ 1 << stride) for i in range(lax.axis_size(axis))])


def split(x):
    hi = x.astype(jnp.bfloat16)
    return hi, (x - hi.astype(jnp.float32)).astype(jnp.bfloat16)


def wide(parts):
    return jnp.concatenate(parts, axis=1)


def tall(parts):
    return jnp.concatenate(parts, axis=0)


def dot(a, b, dims):
    return lax.dot_general(a, b, dims, preferred_element_type=jnp.float32)


def halves(x):
    n = x.shape[1] // 2
    return x[:, :n] + x[:, n:]


def nn(a, b):
    right = wide(b)
    return halves(dot(wide(a), tall((right, right)), NN))


def nt(a, b):
    return halves(dot(wide(a), tall((wide((b[0], b[0])), wide((b[1], b[1])))), NT))


def tn(a, b):
    right = wide(b)
    return halves(dot(tall(a), tall((right, right)), TN))


def fold(x):
    return jnp.sum(x.reshape(x.shape[0] // SUB, SUB, x.shape[1]), axis=0)


def level_table():
    s = lax.broadcasted_iota(jnp.int32, (C, C), 0)
    t = lax.broadcasted_iota(jnp.int32, (C, C), 1)
    x = jnp.bitwise_xor(s, t)
    level = jnp.zeros((C, C), jnp.int32)
    for height in range(C.bit_length() - 1):
        level = level + (x >= 1 << height).astype(jnp.int32)
    return jnp.where(s <= t, level, -1)


def state_kernel(first, bits_ref, q_hbm, k_hbm, v_hbm, d_hbm, w_ref, near_ref, send_ref, keep_ref, left_ref, right_ref, turned_ref, stage_ref, sum_ref, sems):
    heads, frames = left_ref.shape[1:3]
    half = heads // 2
    levels = send_ref.shape[0] + 1
    own = bits_ref[0]

    def copies(head):
        lanes = pl.ds(head * DK, DK)
        return [
            pltpu.make_async_copy(x.at[:, lanes], stage_ref.at[i, head], sems.at[i, head])
            for i, x in enumerate((k_hbm, q_hbm, v_hbm, d_hbm))
        ]

    def prepare(head, span):
        for i in range(2):
            x = stage_ref[i, head, span, :]
            left_ref[i, head, span, :] = wide(split(x))
            turned_ref[i, head, :, span] = x.T
            right_ref[i, head, span, :] = wide(split(stage_ref[2 + i, head, span, :]))

    def products(head, span):
        for level in range(levels):
            bit = bits_ref[level]
            row = jnp.where(bit == 1, w_ref[first + level : first + level + 1, span], 1.0)
            grown = wide(split(row * turned_ref[bit, head, :, span]))
            right = right_ref[bit, head, span, :]
            term = dot(grown, tall((right, right)), NN)
            sum_ref[head, level] = sum_ref[head, level] + term if span.start else term

    for head in range(heads):
        for copy in copies(head):
            copy.start()
    for head in range(heads + 1):
        if head < heads:
            for copy in copies(head):
                copy.wait()
        for b in range(frames // B):
            span = slice(b * B, (b + 1) * B)
            if head < heads:
                prepare(head, span)
            if head:
                products(head - 1, span)
    for head in range(heads):
        near_ref[head] = halves(sum_ref[head, 0])
    for level in range(1, levels):
        for j in range(half):
            low, high = halves(sum_ref[j, level]), halves(sum_ref[half + j, level])
            send_ref[level - 1, j] = jnp.where(own == 0, high, low)
            keep_ref[level - 1, j] = jnp.where(own == 0, low, high)


def upper_pairs(chunks):
    heights = chunks.bit_length() - 1
    return [(c, k) for c in range(chunks) for k in range(heights) if c >> k & 1]


def parts(ref, *at):
    x = ref[at]
    return x[:, :DK], x[:, DK:]


def local_kernel(heads, last, left_ref, right_ref, turned_ref, w_ref, *refs):
    start = heads[0] == 0
    if not start:
        refs = refs[6:]
    qg_ref, kg_ref, vg_ref, pr_ref, wc_ref, mix_ref = refs[:6]
    frames = left_ref.shape[2]
    chunks = frames // C
    heights = chunks.bit_length() - 1
    inner = C.bit_length()
    pairs = upper_pairs(chunks)
    spans = [slice(c * C, (c + 1) * C) for c in range(chunks)]

    if start:
        table = level_table()
        for c in range(chunks):
            mixing = jnp.zeros((C, C), jnp.float32)
            for level in range(inner):
                mixing = jnp.where(table == level, w_ref[level : level + 1, spans[c]], mixing)
            mix_ref[c] = mixing

    def add(head, ref, at, value):
        ref[at] = ref[at] + value if head else value

    def inside(head):
        lanes = slice(head * DK, (head + 1) * DK)
        sums, back = {}, {}
        for c in range(chunks - 1):
            sums[c, 0] = tn(parts(left_ref, 0, head, spans[c]), parts(right_ref, 0, head, spans[c]))
        for k in range(1, heights):
            for b in range(chunks >> k):
                if b << k < chunks - (1 << k):
                    sums[b, k] = sums[2 * b, k - 1] + sums[2 * b + 1, k - 1]

        def scores(c):
            ks, qs = parts(left_ref, 0, head, spans[c]), parts(left_ref, 1, head, spans[c])
            vs, ds = parts(right_ref, 0, head, spans[c]), parts(right_ref, 1, head, spans[c])
            gt = nt(ks, qs)
            et = nt(vs, ds)
            add(head, pr_ref, c, gt * et)
            mt = mix_ref[c]
            return split(mt * et), split(mt * gt)

        def gradients(c, me, mg):
            ks, qs = parts(left_ref, 0, head, spans[c]), parts(left_ref, 1, head, spans[c])
            vs, ds = parts(right_ref, 0, head, spans[c]), parts(right_ref, 1, head, spans[c])
            kg, vg, qg = nn(me, qs), nn(mg, ds), tn(me, ks)
            if c < chunks - 1:
                total = None
                for k in range(heights):
                    if not c >> k & 1:
                        term = back[c >> k, k]
                        total = term if total is None else total + term
                bs = split(total)
                kg = kg + nt(vs, bs)
                vg = vg + nn(ks, bs)
            kg_ref[spans[c], lanes] = kg
            vg_ref[spans[c], lanes] = vg
            ups = [k for k in range(heights) if c >> k & 1]
            if ups:
                qt = turned_ref[1, head, :, spans[c]]
                mixed = None
                for k in ups:
                    row = w_ref[inner + k : inner + k + 1, spans[c]]
                    along = nt(split(sums[(c >> k) - 1, k]), ds)
                    add(head, wc_ref, pairs.index((c, k)), fold(qt * along))
                    term = row * along
                    mixed = term if mixed is None else mixed + term
                    grad = nn(split(row * qt), ds)
                    key = ((c >> k) - 1, k)
                    back[key] = back[key] + grad if key in back else grad
                qg = qg + mixed.T
            qg_ref[spans[c], lanes] = qg

        waiting = None
        for c in reversed(range(chunks)):
            now = scores(c)
            if waiting is not None:
                gradients(c + 1, *waiting)
            waiting = now
        gradients(0, *waiting)

    for head in heads:
        inside(head)

    if last:
        wg_ref = refs[-1]
        table = level_table()
        wg_ref[...] = jnp.zeros_like(wg_ref)
        for c in range(chunks):
            product = pr_ref[c]
            for level in range(inner):
                row = jnp.sum(jnp.where(table == level, product, 0.0), axis=0, keepdims=True)
                wg_ref[level : level + 1, spans[c]] = row
        for i, (c, k) in enumerate(pairs):
            wg_ref[inner + k : inner + k + 1, spans[c]] = jnp.sum(wc_ref[i], axis=0, keepdims=True)


def received(level, head, half, own, refs):
    if level == 0:
        return refs[0][head]
    other, mine = refs[2 * level - 1], refs[2 * level]
    return jnp.where(own == head // half, mine[head % half], other[head % half])


def coarse_kernel(first, levels, final, bits_ref, right_ref, turned_ref, w_ref, qg_ref, *refs):
    count = 2 * levels.stop - 1
    arrived, refs = refs[:count], refs[count:]
    if final:
        out_hbm, wg_ref, wc_ref, out_ref, sems = refs
    else:
        out_ref, wg_ref, wc_ref = refs
    heads, frames = right_ref.shape[1:3]
    lefts = []
    for head in range(heads):
        states = []
        for level in levels:
            state = received(level, head, heads // 2, bits_ref[0], arrived)
            states.append(wide(split(jnp.where(bits_ref[level] == 1, state, 0.0))))
        lefts.append(tall(states))
    for head in range(heads):
        lanes = slice(head * DK, (head + 1) * DK)
        for c in range(frames // C):
            span = slice(c * C, (c + 1) * C)
            dh, dl = parts(right_ref, 1, head, span)
            along = halves(dot(lefts[head], tall((wide((dh, dh)), wide((dl, dl)))), NT))
            qt = turned_ref[1, head, :, span]
            mixed = None
            for i, level in enumerate(levels):
                part = along[i * DK : (i + 1) * DK, :]
                share = fold(qt * part)
                wc_ref[i, :, span] = wc_ref[i, :, span] + share if head else share
                term = w_ref[first + level : first + level + 1, span] * part
                mixed = term if mixed is None else mixed + term
            out_ref[span, lanes] = qg_ref[span, lanes] + mixed.T
        if final:
            pltpu.make_async_copy(out_ref.at[:, lanes], out_hbm.at[:, lanes], sems.at[head]).start()
    for i in range(len(levels)):
        wg_ref[i : i + 1, :] = jnp.sum(wc_ref[i], axis=0, keepdims=True)
    wg_ref[len(levels) :, :] = jnp.zeros((wg_ref.shape[0] - len(levels), frames), jnp.float32)
    if final:
        for head in range(heads):
            lanes = slice(head * DK, (head + 1) * DK)
            pltpu.make_async_copy(out_ref.at[:, lanes], out_hbm.at[:, lanes], sems.at[head]).wait()


def back_kernel(levels, times, bits_ref, left_ref, old_ref, *refs):
    arrived = refs[: 2 * levels - 1]
    out_hbm, out_ref, sems = refs[2 * levels - 1 :]
    heads, frames = left_ref.shape[1:3]
    sums = []
    for head in range(heads):
        total = None
        for level in range(levels):
            state = received(level, head, heads // 2, bits_ref[0], arrived)
            term = jnp.where(bits_ref[level] == 0, state, 0.0)
            total = term if total is None else total + term
        sums.append(split(total))
    for head in range(heads):
        lanes = slice(head * DK, (head + 1) * DK)
        for b in range(frames // B):
            span = slice(b * B, (b + 1) * B)
            out_ref[span, lanes] = old_ref[span, lanes] + times(parts(left_ref, 0, head, span), sums[head])
        pltpu.make_async_copy(out_ref.at[:, lanes], out_hbm.at[:, lanes], sems.at[head]).start()
    for head in range(heads):
        lanes = slice(head * DK, (head + 1) * DK)
        pltpu.make_async_copy(out_ref.at[:, lanes], out_hbm.at[:, lanes], sems.at[head]).wait()


def params(mib):
    return pltpu.CompilerParams(vmem_limit_bytes=mib * 2**20)


def cost(flops, size):
    return pl.CostEstimate(flops=flops, bytes_accessed=size, transcendentals=0)


def groups(heads, windows):
    count = min(heads, windows)
    rest = heads - count + 1
    return [list(range(rest))] + [[rest + i] for i in range(count - 1)]


def body(query_rows, key_rows, value_rows, out_grad, level_weights):
    frames, width = query_rows.shape
    heads = width // DK
    half = heads // 2
    levels = level_weights.shape[0]
    fine = frames.bit_length()
    device_levels = levels - fine
    far = device_levels - 1
    f32, bf16 = jnp.float32, jnp.bfloat16
    big = jax.ShapeDtypeStruct((frames, width), f32)
    kept = pltpu.VMEM((frames, width), f32)
    fine_rows = -(-fine // SUB) * SUB
    chunks = frames // C
    pairs = max(1, len(upper_pairs(chunks)))
    block = frames * width * 4
    device = lax.axis_index("tm")
    bits = jnp.bitwise_and(jnp.right_shift(device, jnp.arange(device_levels)), 1).astype(jnp.int32)
    inputs = [pltpu.with_memory_space_constraint(x, pltpu.HBM) for x in (query_rows, key_rows, value_rows, out_grad)]
    here = pl.BlockSpec(memory_space=pltpu.VMEM)
    there = pl.BlockSpec(memory_space=pl.ANY)
    scalars = pl.BlockSpec(memory_space=pltpu.SMEM)
    far_half = jax.ShapeDtypeStruct((far, half, DK, DK), f32)
    done = pltpu.SemaphoreType.DMA((heads,))

    near, send, keep, left, right, turned = pl.pallas_call(
        functools.partial(state_kernel, fine),
        in_specs=[scalars] + [there] * 4 + [here],
        out_specs=[here] * 6,
        out_shape=[
            jax.ShapeDtypeStruct((heads, DK, DK), f32),
            far_half,
            far_half,
            pltpu.VMEM((2, heads, frames, 2 * DK), bf16),
            pltpu.VMEM((2, heads, frames, 2 * DK), bf16),
            pltpu.VMEM((2, heads, DK, frames), f32),
        ],
        scratch_shapes=[
            pltpu.VMEM((4, heads, frames, DK), f32),
            pltpu.VMEM((heads, device_levels, DK, 2 * DK), f32),
            pltpu.SemaphoreType.DMA((4, heads)),
        ],
        compiler_params=params(16),
        cost_estimate=cost(10**9, 4 * block),
        name="states",
    )(bits, *inputs, level_weights)

    inner = None
    for i, group in enumerate(groups(heads, device_levels)):
        last = group[-1] == heads - 1
        shapes = [kept] * 3
        shapes += [pltpu.VMEM((chunks, C, C), f32), pltpu.VMEM((pairs, SUB, C), f32), pltpu.VMEM((chunks, C, C), f32)]
        inner = pl.pallas_call(
            functools.partial(local_kernel, group, last),
            in_specs=[here] * (10 if i else 4),
            out_specs=[here] * (7 if last else 6),
            out_shape=shapes + ([jax.ShapeDtypeStruct((fine_rows, frames), f32)] if last else []),
            input_output_aliases={4 + j: j for j in range(6)} if i else {},
            compiler_params=params(16),
            cost_estimate=cost(10**9, 7 * block // heads * len(group)),
        )(left, right, turned, level_weights, *(inner or []))
    q_local, k_local, v_local, _, _, _, w_fine = inner

    arrived = []
    carried = keep + partner(send, "tm", 0)
    for height in range(1, device_levels):
        other = partner(carried, "tm", height)
        arrived.append(other[0])
        carried = carried[1:] + other[1:]
    states = [partner(near, "tm", 0)]
    for height in range(far):
        states += [partner(arrived[height], "tm", 0), arrived[height]]

    def coarse(span, query, final):
        used = states[: 2 * span.stop - 1]
        rows = -(-len(span) // SUB) * SUB
        extra = [pltpu.VMEM((frames, width), f32), done] if final else []
        return pl.pallas_call(
            functools.partial(coarse_kernel, fine, span, final),
            in_specs=[scalars] + [here] * (4 + len(used)),
            out_specs=[there if final else here, here],
            out_shape=[big if final else kept, jax.ShapeDtypeStruct((rows, frames), f32)],
            scratch_shapes=[pltpu.VMEM((len(span), SUB, frames), f32)] + extra,
            input_output_aliases={} if final else {4: 0},
            compiler_params=params(16),
            cost_estimate=cost(10**9, 2 * block),
            name="coarse",
        )(bits, right, turned, level_weights, query, *used)

    w_terms = [w_fine[:fine]]
    if far:
        q_local, w_early = coarse(range(far), q_local, False)
        w_terms.append(w_early[:far])
    q_total, w_late = coarse(range(far, device_levels), q_local, True)
    w_terms.append(w_late[:1])

    weight_grad = jnp.concatenate(w_terms, axis=0)
    for height in range(lax.axis_size("head").bit_length() - 1):
        weight_grad = weight_grad + partner(weight_grad, "head", height)

    totals = []
    for times, operand, old in ((nt, right, k_local), (nn, left, v_local)):
        totals.append(
            pl.pallas_call(
                functools.partial(back_kernel, device_levels, times),
                in_specs=[scalars] + [here] * (2 + len(states)),
                out_specs=there,
                out_shape=big,
                scratch_shapes=[pltpu.VMEM((frames, width), f32), done],
                compiler_params=params(16),
                cost_estimate=cost(10**9, 2 * block),
            )(bits, operand, old, *states)
        )
    return (q_total, *totals, weight_grad)


def solution(mesh):
    in_specs = (P("tm", "head"), P("tm", "head"), P("tm", "head"), P("tm", "head"), P(None, "tm"))
    out_specs = (P("tm", "head"), P("tm", "head"), P("tm", "head"), P(None, "tm"))
    return jax.shard_map(body, mesh=mesh, in_specs=in_specs, out_specs=out_specs, check_vma=False)
```

```python
import functools

import jax
import jax.numpy as jnp
from jax import lax
from jax.experimental import pallas as pl
from jax.experimental.pallas import tpu as pltpu
from jax.sharding import PartitionSpec as P


DK = 128
C = 128
B = 256
SUB = 8
NN = (((1,), (0,)), ((), ()))
NT = (((1,), (1,)), ((), ()))
TN = (((0,), (0,)), ((), ()))


def partner(array, axis, stride):
    return lax.ppermute(array, axis, [(i, i ^ 1 << stride) for i in range(lax.axis_size(axis))])


def split(x):
    hi = x.astype(jnp.bfloat16)
    return hi, (x - hi.astype(jnp.float32)).astype(jnp.bfloat16)


def wide(parts):
    return jnp.concatenate(parts, axis=1)


def tall(parts):
    return jnp.concatenate(parts, axis=0)


def dot(a, b, dims):
    return lax.dot_general(a, b, dims, preferred_element_type=jnp.float32)


def halves(x):
    n = x.shape[1] // 2
    return x[:, :n] + x[:, n:]


def nn(a, b):
    right = wide(b)
    return halves(dot(wide(a), tall((right, right)), NN))


def nt(a, b):
    return halves(dot(wide(a), tall((wide((b[0], b[0])), wide((b[1], b[1])))), NT))


def tn(a, b):
    right = wide(b)
    return halves(dot(tall(a), tall((right, right)), TN))


def fold(x):
    return jnp.sum(x.reshape(x.shape[0] // SUB, SUB, x.shape[1]), axis=0)


def level_table():
    s = lax.broadcasted_iota(jnp.int32, (C, C), 0)
    t = lax.broadcasted_iota(jnp.int32, (C, C), 1)
    x = jnp.bitwise_xor(s, t)
    level = jnp.zeros((C, C), jnp.int32)
    for height in range(C.bit_length() - 1):
        level = level + (x >= 1 << height).astype(jnp.int32)
    return jnp.where(s <= t, level, -1)


def bit_of(level):
    return jnp.bitwise_and(jnp.right_shift(lax.axis_index("tm"), level), 1)


def state_kernel(first, q_hbm, k_hbm, v_hbm, d_hbm, w_hbm, near_ref, send_ref, keep_ref, left_ref, right_refs, turned_refs, w_ref, stage_ref, sum_ref, sems, w_sem):
    heads, frames = left_ref.shape[1:3]
    half = heads // 2
    levels = send_ref.shape[0] + 1
    own = bit_of(0)

    def copies(head):
        lanes = pl.ds(head * DK, DK)
        return [
            pltpu.make_async_copy(x.at[:, lanes], stage_ref.at[i, head], sems.at[i, head])
            for i, x in enumerate((k_hbm, q_hbm, v_hbm, d_hbm))
        ]

    def prepare(head, span):
        for i in range(2):
            x = stage_ref[i, head, span, :]
            left_ref[i, head, span, :] = wide(split(x))
            turned_refs[head % 2][i, head // 2, :, span] = x.T
            right_refs[head % 2][i, head // 2, span, :] = wide(split(stage_ref[2 + i, head, span, :]))

    def products(head, span):
        for level in range(levels):
            bit = bit_of(level)
            row = jnp.where(bit == 1, w_ref[first + level : first + level + 1, span], 1.0)
            grown = wide(split(row * turned_refs[head % 2][bit, head // 2, :, span]))
            right = right_refs[head % 2][bit, head // 2, span, :]
            term = dot(grown, tall((right, right)), NN)
            sum_ref[head, level] = sum_ref[head, level] + term if span.start else term

    weights = pltpu.make_async_copy(w_hbm, w_ref, w_sem)
    for head in range(heads):
        for copy in copies(head):
            copy.start()
        if head == 0:
            weights.start()
    for head in range(heads + 1):
        if head < heads:
            for copy in copies(head):
                copy.wait()
        if head == 1:
            weights.wait()
        for b in range(frames // B):
            span = slice(b * B, (b + 1) * B)
            if head < heads:
                prepare(head, span)
            if head:
                products(head - 1, span)
    for head in range(heads):
        near_ref[head] = halves(sum_ref[head, 0])
    for level in range(1, levels):
        for j in range(half):
            low, high = halves(sum_ref[j, level]), halves(sum_ref[half + j, level])
            send_ref[level - 1, j] = jnp.where(own == 0, high, low)
            keep_ref[level - 1, j] = jnp.where(own == 0, low, high)


def upper_pairs(chunks):
    heights = chunks.bit_length() - 1
    return [(c, k) for c in range(chunks) for k in range(heights) if c >> k & 1]


def parts(ref, *at):
    x = ref[at]
    return x[:, :DK], x[:, DK:]


def local_kernel(heads, last, left_ref, right_refs, turned_refs, w_ref, *refs):
    start = heads[0] == 0
    if not start:
        refs = refs[7:]
    qg_ref, kg_ref, vg_ref, pr_ref, wc_ref, mix_ref, col_ref = refs[:7]
    frames = left_ref.shape[2]
    chunks = frames // C
    heights = chunks.bit_length() - 1
    inner = C.bit_length()
    pairs = upper_pairs(chunks)
    spans = [slice(c * C, (c + 1) * C) for c in range(chunks)]

    if start:
        table = level_table()
        for c in range(chunks):
            mixing = jnp.zeros((C, C), jnp.float32)
            for level in range(inner):
                mixing = jnp.where(table == level, w_ref[level : level + 1, spans[c]], mixing)
            mix_ref[c] = mixing
            for i in range(col_ref.shape[0]):
                level = inner + heights + i
                col_ref[i, spans[c], :] = jnp.broadcast_to(w_ref[level : level + 1, spans[c]], (C, C)).T

    def right(i, head, span):
        return parts(right_refs[head % 2], i, head // 2, span)

    def add(head, ref, at, value):
        ref[at] = ref[at] + value if head else value

    def inside(head):
        lanes = slice(head * DK, (head + 1) * DK)
        sums, back = {}, {}
        for c in range(chunks - 1):
            sums[c, 0] = tn(parts(left_ref, 0, head, spans[c]), right(0, head, spans[c]))
        for k in range(1, heights):
            for b in range(chunks >> k):
                if b << k < chunks - (1 << k):
                    sums[b, k] = sums[2 * b, k - 1] + sums[2 * b + 1, k - 1]

        def scores(c):
            ks, qs = parts(left_ref, 0, head, spans[c]), parts(left_ref, 1, head, spans[c])
            vs, ds = right(0, head, spans[c]), right(1, head, spans[c])
            gt = nt(ks, qs)
            et = nt(vs, ds)
            add(head, pr_ref, c, gt * et)
            mt = mix_ref[c]
            return split(mt * et), split(mt * gt)

        def gradients(c, me, mg):
            ks, qs = parts(left_ref, 0, head, spans[c]), parts(left_ref, 1, head, spans[c])
            vs, ds = right(0, head, spans[c]), right(1, head, spans[c])
            kg, vg, qg = nn(me, qs), nn(mg, ds), tn(me, ks)
            if c < chunks - 1:
                total = None
                for k in range(heights):
                    if not c >> k & 1:
                        term = back[c >> k, k]
                        total = term if total is None else total + term
                bs = split(total)
                kg = kg + nt(vs, bs)
                vg = vg + nn(ks, bs)
            kg_ref[spans[c], lanes] = kg
            vg_ref[spans[c], lanes] = vg
            ups = [k for k in range(heights) if c >> k & 1]
            if ups:
                qt = turned_refs[head % 2][1, head // 2, :, spans[c]]
                mixed = None
                for k in ups:
                    row = w_ref[inner + k : inner + k + 1, spans[c]]
                    along = nt(split(sums[(c >> k) - 1, k]), ds)
                    add(head, wc_ref, pairs.index((c, k)), fold(qt * along))
                    term = row * along
                    mixed = term if mixed is None else mixed + term
                    grad = nn(split(row * qt), ds)
                    key = ((c >> k) - 1, k)
                    back[key] = back[key] + grad if key in back else grad
                qg = qg + mixed.T
            qg_ref[spans[c], lanes] = qg

        waiting = None
        for c in reversed(range(chunks)):
            now = scores(c)
            if waiting is not None:
                gradients(c + 1, *waiting)
            waiting = now
        gradients(0, *waiting)

    for head in heads:
        inside(head)

    if last:
        wg_ref = refs[7]
        table = level_table()
        wg_ref[...] = jnp.zeros_like(wg_ref)
        for c in range(chunks):
            product = pr_ref[c]
            for level in range(inner):
                row = jnp.sum(jnp.where(table == level, product, 0.0), axis=0, keepdims=True)
                wg_ref[level : level + 1, spans[c]] = row
        for i, (c, k) in enumerate(pairs):
            wg_ref[inner + k : inner + k + 1, spans[c]] = jnp.sum(wc_ref[i], axis=0, keepdims=True)


def received(level, head, half, refs):
    if level == 0:
        return refs[0][head]
    other, mine = refs[2 * level - 1], refs[2 * level]
    return jnp.where(bit_of(0) == head // half, mine[head % half], other[head % half])


def coarse_kernel(first, levels, left_ref, right_refs, col_ref, old_q, old_w, *refs):
    count = 2 * levels.stop - 1
    arrived = refs[:count]
    out_ref, wg_ref, product_ref = refs[count:]
    heads, frames = left_ref.shape[1:3]
    for head in range(heads):
        lanes = slice(head * DK, (head + 1) * DK)
        states = []
        for level in levels:
            state = received(level, head, heads // 2, arrived)
            states.append(split(jnp.where(bit_of(level) == 1, state, 0.0)))
        for b in range(frames // B):
            span = slice(b * B, (b + 1) * B)
            ds = parts(right_refs[head % 2], 1, head // 2, span)
            qh, ql = parts(left_ref, 1, head, span)
            q = qh.astype(jnp.float32) + ql.astype(jnp.float32)
            mixed = old_q[span, lanes]
            for i, level in enumerate(levels):
                along = nt(ds, states[i])
                product_ref[i, span, :] = product_ref[i, span, :] + q * along if head else q * along
                mixed = mixed + col_ref[level, span, :] * along
            out_ref[span, lanes] = mixed
    for i, level in enumerate(levels):
        for c in range(frames // C):
            span = slice(c * C, (c + 1) * C)
            row = jnp.sum(product_ref[i, span, :].T, axis=0, keepdims=True)
            wg_ref[first + level : first + level + 1, span] = row


def back_kernel(levels, times, operand, extra, *refs):
    if operand == "left":
        factor = lambda head, span, ref: parts(ref, 0, head, span)
        factor_refs, refs = refs[0], refs[1:]
    else:
        factor = lambda head, span, refs: parts(refs[head % 2], 0, head // 2, span)
        factor_refs, refs = refs[0], refs[1:]
    old_ref, refs = refs[0], refs[1:]
    whole = []
    if extra:
        done_ref, refs = refs[0], refs[1:]
    arrived, refs = refs[: 2 * levels - 1], refs[2 * levels - 1 :]
    out_hbm, refs = refs[0], refs[1:]
    if extra:
        done_hbm, refs = refs[0], refs[1:]
    out_ref, sems = refs
    frames, width = old_ref.shape
    heads = width // DK
    blocks = frames // B
    if extra:
        whole = [pltpu.make_async_copy(done_ref, done_hbm, sems.at[heads, 0])]
        whole[0].start()

    def copy(head, b):
        at = (slice(b * B, (b + 1) * B), slice(head * DK, (head + 1) * DK))
        return pltpu.make_async_copy(out_ref.at[at], out_hbm.at[at], sems.at[head, b])

    for head in range(heads):
        lanes = slice(head * DK, (head + 1) * DK)
        total = None
        for level in range(levels):
            state = received(level, head, heads // 2, arrived)
            term = jnp.where(bit_of(level) == 0, state, 0.0)
            total = term if total is None else total + term
        bs = split(total)
        for b in range(blocks):
            span = slice(b * B, (b + 1) * B)
            out_ref[span, lanes] = old_ref[span, lanes] + times(factor(head, span, factor_refs), bs)
            copy(head, b).start()
    for head in range(heads):
        for b in range(blocks):
            copy(head, b).wait()
    for item in whole:
        item.wait()


def params(mib):
    return pltpu.CompilerParams(vmem_limit_bytes=mib * 2**20)


def cost(flops, size):
    return pl.CostEstimate(flops=flops, bytes_accessed=size, transcendentals=0)


def groups(heads, windows):
    count = min(heads, windows)
    rest = heads - count + 1
    return [list(range(rest))] + [[rest + i] for i in range(count - 1)]


def body(query_rows, key_rows, value_rows, out_grad, level_weights):
    frames, width = query_rows.shape
    heads = width // DK
    half = heads // 2
    levels = level_weights.shape[0]
    fine = frames.bit_length()
    device_levels = levels - fine
    far = device_levels - 1
    f32, bf16 = jnp.float32, jnp.bfloat16
    big = jax.ShapeDtypeStruct((frames, width), f32)
    kept = pltpu.VMEM((frames, width), f32)
    chunks = frames // C
    pairs = max(1, len(upper_pairs(chunks)))
    block = frames * width * 4
    here = pl.BlockSpec(memory_space=pltpu.VMEM)
    there = pl.BlockSpec(memory_space=pl.ANY)
    inputs = [pltpu.with_memory_space_constraint(x, pltpu.HBM) for x in (query_rows, key_rows, value_rows, out_grad, level_weights)]
    far_half = jax.ShapeDtypeStruct((far, half, DK, DK), f32)
    rows = -(-levels // SUB) * SUB

    near, send, keep, left, right, turned = pl.pallas_call(
        functools.partial(state_kernel, fine),
        in_specs=[there] * 5,
        out_specs=[here] * 4 + [[here] * 2] * 2,
        out_shape=[
            jax.ShapeDtypeStruct((heads, DK, DK), f32),
            far_half,
            far_half,
            pltpu.VMEM((2, heads, frames, 2 * DK), bf16),
            [pltpu.VMEM((2, half, frames, 2 * DK), bf16)] * 2,
            [pltpu.VMEM((2, half, DK, frames), f32)] * 2,
        ],
        scratch_shapes=[
            pltpu.VMEM((levels, frames), f32),
            pltpu.VMEM((4, heads, frames, DK), f32),
            pltpu.VMEM((heads, device_levels, DK, 2 * DK), f32),
            pltpu.SemaphoreType.DMA((4, heads)),
            pltpu.SemaphoreType.DMA,
        ],
        compiler_params=params(16),
        cost_estimate=cost(10**9, 4 * block),
        name="states",
    )(*inputs)

    inner = None
    for i, group in enumerate(groups(heads, device_levels)):
        last = group[-1] == heads - 1
        shapes = [kept] * 3
        shapes += [pltpu.VMEM((chunks, C, C), f32), pltpu.VMEM((pairs, SUB, C), f32), pltpu.VMEM((chunks, C, C), f32)]
        shapes.append(pltpu.VMEM((device_levels, frames, DK), f32))
        if last:
            shapes.append(pltpu.VMEM((rows, frames), f32))
        inner = pl.pallas_call(
            functools.partial(local_kernel, group, last),
            in_specs=[here] + [[here] * 2] * 2 + [here] * (8 if i else 1),
            out_specs=[here] * len(shapes),
            out_shape=shapes,
            input_output_aliases={6 + j: j for j in range(7)} if i else {},
            compiler_params=params(16),
            cost_estimate=cost(10**9, 7 * block // heads * len(group)),
        )(left, right, turned, level_weights, *(inner or []))
    q_local, k_local, v_local, _, _, _, columns, weight_grad = inner

    arrived = []
    carried = keep + partner(send, "tm", 0)
    for height in range(1, device_levels):
        other = partner(carried, "tm", height)
        arrived.append(other[0])
        carried = carried[1:] + other[1:]
    states = [partner(near, "tm", 0)]
    for height in range(far):
        states += [partner(arrived[height], "tm", 0), arrived[height]]

    def coarse(span, query, weight):
        used = states[: 2 * span.stop - 1]
        return pl.pallas_call(
            functools.partial(coarse_kernel, fine, span),
            in_specs=[here, [here] * 2] + [here] * (3 + len(used)),
            out_specs=[here] * 2,
            out_shape=[kept, pltpu.VMEM((rows, frames), f32)],
            scratch_shapes=[pltpu.VMEM((len(span), frames, DK), f32)],
            input_output_aliases={4: 0, 5: 1},
            compiler_params=params(16),
            cost_estimate=cost(10**9, 2 * block),
            name="coarse",
        )(left, right, columns, query, weight, *used)

    if far:
        q_local, weight_grad = coarse(range(far), q_local, weight_grad)
    q_local, weight_grad = coarse(range(far, device_levels), q_local, weight_grad)
    for height in range(lax.axis_size("head").bit_length() - 1):
        weight_grad = weight_grad + partner(weight_grad, "head", height)

    def back(times, operand, factor, old, extra):
        return pl.pallas_call(
            functools.partial(back_kernel, device_levels, times, operand, bool(extra)),
            in_specs=[here if operand == "left" else [here] * 2] + [here] * (1 + len(extra) + len(states)),
            out_specs=[there] * (1 + len(extra)),
            out_shape=[big] * (1 + len(extra)),
            scratch_shapes=[
                pltpu.VMEM((frames, width), f32),
                pltpu.SemaphoreType.DMA((heads + 1, frames // B)),
            ],
            compiler_params=params(16),
            cost_estimate=cost(10**9, 2 * block),
        )(factor, old, *extra, *states)

    (k_total,) = back(nt, "right", right, k_local, [])
    v_total, q_total = back(nn, "left", left, v_local, [q_local])
    return (q_total, k_total, v_total, weight_grad[:levels])


def solution(mesh):
    in_specs = (P("tm", "head"), P("tm", "head"), P("tm", "head"), P("tm", "head"), P(None, "tm"))
    out_specs = (P("tm", "head"), P("tm", "head"), P("tm", "head"), P(None, "tm"))
    return jax.shard_map(body, mesh=mesh, in_specs=in_specs, out_specs=out_specs, check_vma=False)
```

```python
import functools

import jax
import jax.numpy as jnp
from jax import lax
from jax.experimental import pallas as pl
from jax.experimental.pallas import tpu as pltpu
from jax.sharding import PartitionSpec as P


DK = 128
C = 128
B = 256
SUB = 8
NN = (((1,), (0,)), ((), ()))
NT = (((1,), (1,)), ((), ()))
TN = (((0,), (0,)), ((), ()))


def partner(array, axis, stride):
    return lax.ppermute(array, axis, [(i, i ^ 1 << stride) for i in range(lax.axis_size(axis))])


def split(x):
    hi = x.astype(jnp.bfloat16)
    return hi, (x - hi.astype(jnp.float32)).astype(jnp.bfloat16)


def wide(parts):
    return jnp.concatenate(parts, axis=1)


def tall(parts):
    return jnp.concatenate(parts, axis=0)


def dot(a, b, dims):
    return lax.dot_general(a, b, dims, preferred_element_type=jnp.float32)


def halves(x):
    n = x.shape[1] // 2
    return x[:, :n] + x[:, n:]


def nn(a, b):
    right = wide(b)
    return halves(dot(wide(a), tall((right, right)), NN))


def nt(a, b):
    return halves(dot(wide(a), tall((wide((b[0], b[0])), wide((b[1], b[1])))), NT))


def tn(a, b):
    right = wide(b)
    return halves(dot(tall(a), tall((right, right)), TN))


def fold(x):
    return jnp.sum(x.reshape(x.shape[0] // SUB, SUB, x.shape[1]), axis=0)


def level_table():
    s = lax.broadcasted_iota(jnp.int32, (C, C), 0)
    t = lax.broadcasted_iota(jnp.int32, (C, C), 1)
    x = jnp.bitwise_xor(s, t)
    level = jnp.zeros((C, C), jnp.int32)
    for height in range(C.bit_length() - 1):
        level = level + (x >= 1 << height).astype(jnp.int32)
    return jnp.where(s <= t, level, -1)


def bit_of(level):
    return jnp.bitwise_and(jnp.right_shift(lax.axis_index("tm"), level), 1)


def halving_bit(level):
    return min(level, 2) - 1


def product(bit, row, turned, rights):
    grown = wide(split(jnp.where(bit == 1, row * turned[1], turned[0])))
    right = jnp.where(bit == 1, rights[1], rights[0])
    return dot(grown, tall((right, right)), NN)


def state_kernel(first, levels, k_hbm, q_hbm, v_hbm, d_hbm, w_hbm, send_refs, keep_refs, kq_ref, right_ref, turned_ref, w_ref, stage_ref, sum_ref, sems, w_sem):
    heads, frames = kq_ref.shape[1:3]
    half = heads // 2

    def copies(head):
        lanes = pl.ds(head * DK, DK)
        ends = (kq_ref.at[0, head], kq_ref.at[1, head], stage_ref.at[0, head], stage_ref.at[1, head])
        return [
            pltpu.make_async_copy(x.at[:, lanes], end, sems.at[i, head])
            for i, (x, end) in enumerate(zip((k_hbm, q_hbm, v_hbm, d_hbm), ends))
        ]

    def start(head):
        if head < heads:
            for copy in copies(head):
                copy.start()

    weights = pltpu.make_async_copy(w_hbm, w_ref, w_sem)
    weights.start()
    start(0)
    start(1)
    weights.wait()
    for head in range(heads):
        for copy in copies(head):
            copy.wait()
        start(head + 2)
        for b in range(frames // B):
            span = slice(b * B, (b + 1) * B)
            turned, rights = [], []
            for i in range(2):
                turned.append(kq_ref[i, head, span, :].T)
                rights.append(wide(split(stage_ref[i, head, span, :])))
                turned_ref[i, head, :, span] = turned[i]
                right_ref[i, head, span, :] = rights[i]
            for level in range(1, levels):
                row = w_ref[first + level : first + level + 1, span]
                term = product(bit_of(level), row, turned, rights)
                sum_ref[head, level - 1] = sum_ref[head, level - 1] + term if b else term
    for level in range(1, levels):
        own = bit_of(halving_bit(level))
        for j in range(half):
            low, high = halves(sum_ref[j, level - 1]), halves(sum_ref[half + j, level - 1])
            send_refs[level - 1][j] = jnp.where(own == 0, high, low)
            keep_refs[level - 1][j] = jnp.where(own == 0, low, high)


def near_kernel(first, right_ref, turned_ref, w_ref, near_ref):
    heads, frames = right_ref.shape[1:3]
    for head in range(heads):
        total = None
        for b in range(frames // B):
            span = slice(b * B, (b + 1) * B)
            turned = [turned_ref[i, head, :, span] for i in range(2)]
            rights = [right_ref[i, head, span, :] for i in range(2)]
            term = product(bit_of(0), w_ref[first : first + 1, span], turned, rights)
            total = term if total is None else total + term
        near_ref[head] = halves(total)


def upper_pairs(chunks):
    heights = chunks.bit_length() - 1
    return [(c, k) for c in range(chunks) for k in range(heights) if c >> k & 1]


def parts(ref, *at):
    x = ref[at]
    return x[:, :DK], x[:, DK:]


def local_kernel(heads, last, kq_ref, right_ref, turned_ref, w_ref, *refs):
    start = heads[0] == 0
    if not start:
        refs = refs[7:]
    qg_ref, kg_ref, vg_ref, pr_ref, wc_ref, mix_ref, col_ref = refs[:7]
    left_ref = refs[-1]
    frames = kq_ref.shape[2]
    chunks = frames // C
    heights = chunks.bit_length() - 1
    inner = C.bit_length()
    pairs = upper_pairs(chunks)
    spans = [slice(c * C, (c + 1) * C) for c in range(chunks)]

    if start:
        table = level_table()
        for c in range(chunks):
            mixing = jnp.zeros((C, C), jnp.float32)
            for level in range(inner):
                mixing = jnp.where(table == level, w_ref[level : level + 1, spans[c]], mixing)
            mix_ref[c] = mixing
            for i in range(col_ref.shape[0]):
                level = inner + heights + i
                col_ref[i, spans[c], :] = jnp.broadcast_to(w_ref[level : level + 1, spans[c]], (C, C)).T

    def right(i, head, span):
        return parts(right_ref, i, head, span)

    def add(head, ref, at, value):
        ref[at] = ref[at] + value if head else value

    def inside(head):
        lanes = slice(head * DK, (head + 1) * DK)
        sums, back = {}, {}
        place = head - heads[0]
        for c in range(chunks):
            for i in range(2):
                left_ref[place, i, spans[c], :] = wide(split(kq_ref[i, head, spans[c], :]))
        for c in range(chunks - 1):
            sums[c, 0] = tn(parts(left_ref, place, 0, spans[c]), right(0, head, spans[c]))
        for k in range(1, heights):
            for b in range(chunks >> k):
                if b << k < chunks - (1 << k):
                    sums[b, k] = sums[2 * b, k - 1] + sums[2 * b + 1, k - 1]

        def scores(c):
            ks, qs = parts(left_ref, place, 0, spans[c]), parts(left_ref, place, 1, spans[c])
            vs, ds = right(0, head, spans[c]), right(1, head, spans[c])
            gt = nt(ks, qs)
            et = nt(vs, ds)
            add(head, pr_ref, c, gt * et)
            mt = mix_ref[c]
            return split(mt * et), split(mt * gt)

        def gradients(c, me, mg):
            ks, qs = parts(left_ref, place, 0, spans[c]), parts(left_ref, place, 1, spans[c])
            vs, ds = right(0, head, spans[c]), right(1, head, spans[c])
            kg, vg, qg = nn(me, qs), nn(mg, ds), tn(me, ks)
            if c < chunks - 1:
                total = None
                for k in range(heights):
                    if not c >> k & 1:
                        term = back[c >> k, k]
                        total = term if total is None else total + term
                bs = split(total)
                kg = kg + nt(vs, bs)
                vg = vg + nn(ks, bs)
            kg_ref[spans[c], lanes] = kg
            vg_ref[spans[c], lanes] = vg
            ups = [k for k in range(heights) if c >> k & 1]
            if ups:
                qt = turned_ref[1, head, :, spans[c]]
                mixed = None
                for k in ups:
                    row = w_ref[inner + k : inner + k + 1, spans[c]]
                    along = nt(split(sums[(c >> k) - 1, k]), ds)
                    add(head, wc_ref, pairs.index((c, k)), fold(qt * along))
                    term = row * along
                    mixed = term if mixed is None else mixed + term
                    grad = nn(split(row * qt), ds)
                    key = ((c >> k) - 1, k)
                    back[key] = back[key] + grad if key in back else grad
                qg = qg + mixed.T
            qg_ref[spans[c], lanes] = qg

        waiting = None
        for c in reversed(range(chunks)):
            now = scores(c)
            if waiting is not None:
                gradients(c + 1, *waiting)
            waiting = now
        gradients(0, *waiting)

    for head in heads:
        inside(head)

    if last:
        wg_ref = refs[7]
        table = level_table()
        wg_ref[...] = jnp.zeros_like(wg_ref)
        for c in range(chunks):
            product = pr_ref[c]
            for level in range(inner):
                row = jnp.sum(jnp.where(table == level, product, 0.0), axis=0, keepdims=True)
                wg_ref[level : level + 1, spans[c]] = row
        for i, (c, k) in enumerate(pairs):
            wg_ref[inner + k : inner + k + 1, spans[c]] = jnp.sum(wc_ref[i], axis=0, keepdims=True)


def received(level, head, half, refs):
    if level == 0:
        return refs[0][head]
    other, mine = refs[2 * level - 1], refs[2 * level]
    return jnp.where(bit_of(halving_bit(level)) == head // half, mine[head % half], other[head % half])


def coarse_kernel(first, levels, kq_ref, right_ref, col_ref, old_q, old_w, *refs):
    arrived, (out_ref, wg_ref, product_ref) = refs[:-3], refs[-3:]
    heads, frames = kq_ref.shape[1:3]
    arrived = [None] * (2 * levels[-1] + 1 - len(arrived)) + list(arrived)
    for head in range(heads):
        lanes = slice(head * DK, (head + 1) * DK)
        states = []
        for level in levels:
            state = received(level, head, heads // 2, arrived)
            states.append(split(jnp.where(bit_of(level) == 1, state, 0.0)))
        for b in range(frames // B):
            span = slice(b * B, (b + 1) * B)
            ds = parts(right_ref, 1, head, span)
            q = kq_ref[1, head, span, :]
            mixed = old_q[span, lanes]
            for i, level in enumerate(levels):
                along = nt(ds, states[i])
                product_ref[i, span, :] = product_ref[i, span, :] + q * along if head else q * along
                mixed = mixed + col_ref[level, span, :] * along
            out_ref[span, lanes] = mixed
    for i, level in enumerate(levels):
        for c in range(frames // C):
            span = slice(c * C, (c + 1) * C)
            row = jnp.sum(product_ref[i, span, :].T, axis=0, keepdims=True)
            wg_ref[first + level : first + level + 1, span] = row


def back_kernel(levels, kq_ref, right_ref, old_k, old_v, q_ref, *refs):
    arrived = refs[: 2 * levels - 1]
    k_hbm, v_hbm, q_hbm, k_ref, v_ref, sems, q_sem = refs[2 * levels - 1 :]
    heads, frames = kq_ref.shape[1:3]
    blocks = frames // B
    queries = pltpu.make_async_copy(q_ref, q_hbm, q_sem)
    queries.start()

    def copies(head, b):
        at = (slice(b * B, (b + 1) * B), slice(head * DK, (head + 1) * DK))
        return [
            pltpu.make_async_copy(x.at[at], end.at[at], sems.at[i, head, b])
            for i, (x, end) in enumerate(((k_ref, k_hbm), (v_ref, v_hbm)))
        ]

    for head in range(heads):
        lanes = slice(head * DK, (head + 1) * DK)
        total = None
        for level in range(levels):
            state = received(level, head, heads // 2, arrived)
            term = jnp.where(bit_of(level) == 0, state, 0.0)
            total = term if total is None else total + term
        bs = split(total)
        for b in range(blocks):
            span = slice(b * B, (b + 1) * B)
            k_ref[span, lanes] = old_k[span, lanes] + nt(parts(right_ref, 0, head, span), bs)
            v_ref[span, lanes] = old_v[span, lanes] + nn(split(kq_ref[0, head, span, :]), bs)
            for copy in copies(head, b):
                copy.start()
    for head in range(heads):
        for b in range(blocks):
            for copy in copies(head, b):
                copy.wait()
    queries.wait()


def params(mib):
    return pltpu.CompilerParams(vmem_limit_bytes=mib * 2**20)


def cost(flops, size):
    return pl.CostEstimate(flops=flops, bytes_accessed=size, transcendentals=0)


def body(query_rows, key_rows, value_rows, out_grad, level_weights):
    frames, width = query_rows.shape
    heads = width // DK
    half = heads // 2
    levels = level_weights.shape[0]
    fine = frames.bit_length()
    device_levels = levels - fine
    far = device_levels - 1
    f32, bf16 = jnp.float32, jnp.bfloat16
    big = jax.ShapeDtypeStruct((frames, width), f32)
    kept = pltpu.VMEM((frames, width), f32)
    chunks = frames // C
    pairs = max(1, len(upper_pairs(chunks)))
    block = frames * width * 4
    here = pl.BlockSpec(memory_space=pltpu.VMEM)
    there = pl.BlockSpec(memory_space=pl.ANY)
    inputs = [pltpu.with_memory_space_constraint(x, pltpu.HBM) for x in (query_rows, key_rows, value_rows, out_grad, level_weights)]
    part = jax.ShapeDtypeStruct((half, DK, DK), f32)
    rows = -(-levels // SUB) * SUB

    send, keep, kq, right, turned = pl.pallas_call(
        functools.partial(state_kernel, fine, device_levels),
        in_specs=[there] * 5,
        out_specs=[[here] * far] * 2 + [here] * 3,
        out_shape=[
            [part] * far,
            [part] * far,
            pltpu.VMEM((2, heads, frames, DK), f32),
            pltpu.VMEM((2, heads, frames, 2 * DK), bf16),
            pltpu.VMEM((2, heads, DK, frames), f32),
        ],
        scratch_shapes=[
            pltpu.VMEM((levels, frames), f32),
            pltpu.VMEM((2, heads, frames, DK), f32),
            pltpu.VMEM((heads, far, DK, 2 * DK), f32),
            pltpu.SemaphoreType.DMA((4, heads)),
            pltpu.SemaphoreType.DMA,
        ],
        compiler_params=params(16),
        cost_estimate=cost(10**9, 4 * block),
        name="states",
    )(inputs[1], inputs[0], *inputs[2:])

    near = pl.pallas_call(
        functools.partial(near_kernel, fine),
        in_specs=[here] * 3,
        out_specs=here,
        out_shape=jax.ShapeDtypeStruct((heads, DK, DK), f32),
        compiler_params=params(16),
        cost_estimate=cost(10**9, block),
        name="near",
    )(right, turned, level_weights)

    inner = None
    for head in range(heads):
        last = head == heads - 1
        shapes = [kept] * 3
        shapes += [pltpu.VMEM((chunks, C, C), f32), pltpu.VMEM((pairs, SUB, C), f32), pltpu.VMEM((chunks, C, C), f32)]
        shapes.append(pltpu.VMEM((device_levels, frames, DK), f32))
        if last:
            shapes.append(pltpu.VMEM((rows, frames), f32))
        inner = pl.pallas_call(
            functools.partial(local_kernel, [head], last),
            in_specs=[here] * (11 if head else 4),
            out_specs=[here] * len(shapes),
            out_shape=shapes,
            scratch_shapes=[pltpu.VMEM((1, 2, frames, 2 * DK), bf16)],
            input_output_aliases={4 + j: j for j in range(7)} if head else {},
            compiler_params=params(16),
            cost_estimate=cost(10**9, 7 * block // heads),
        )(kq, right, turned, level_weights, *(inner or []))
    q_local, k_local, v_local, _, _, _, columns, weight_grad = inner

    states = [partner(near, "tm", 0)]
    for level in range(1, device_levels):
        halver = halving_bit(level)
        carried = keep[level - 1] + partner(send[level - 1], "tm", halver)
        for height in range(level):
            if height != halver:
                carried = carried + partner(carried, "tm", height)
        carried = partner(carried, "tm", level)
        states += [partner(carried, "tm", halver), carried]

    def coarse(span, query, weight):
        used = states[max(0, 2 * span[0] - 1) : 2 * span[-1] + 1]
        return pl.pallas_call(
            functools.partial(coarse_kernel, fine, span),
            in_specs=[here] * (5 + len(used)),
            out_specs=[here] * 2,
            out_shape=[kept, pltpu.VMEM((rows, frames), f32)],
            scratch_shapes=[pltpu.VMEM((len(span), frames, DK), f32)],
            input_output_aliases={3: 0, 4: 1},
            compiler_params=params(16),
            cost_estimate=cost(10**9, 2 * block),
            name="coarse",
        )(kq, right, columns, query, weight, *used)

    q_local, weight_grad = coarse(list(range(far)), q_local, weight_grad)
    q_local, weight_grad = coarse([far], q_local, weight_grad)
    for height in range(lax.axis_size("head").bit_length() - 1):
        weight_grad = weight_grad + partner(weight_grad, "head", height)

    k_total, v_total, q_total = pl.pallas_call(
        functools.partial(back_kernel, device_levels),
        in_specs=[here] * (5 + len(states)),
        out_specs=[there] * 3,
        out_shape=[big] * 3,
        scratch_shapes=[
            pltpu.VMEM((frames, width), f32),
            pltpu.VMEM((frames, width), f32),
            pltpu.SemaphoreType.DMA((2, heads, frames // B)),
            pltpu.SemaphoreType.DMA,
        ],
        compiler_params=params(16),
        cost_estimate=cost(10**9, 4 * block),
        name="back",
    )(kq, right, k_local, v_local, q_local, *states)
    return (q_total, k_total, v_total, weight_grad[:levels])


def solution(mesh):
    in_specs = (P("tm", "head"), P("tm", "head"), P("tm", "head"), P("tm", "head"), P(None, "tm"))
    out_specs = (P("tm", "head"), P("tm", "head"), P("tm", "head"), P(None, "tm"))
    return jax.shard_map(body, mesh=mesh, in_specs=in_specs, out_specs=out_specs, check_vma=False)
```

```python
import functools

import jax
import jax.numpy as jnp
from jax import lax
from jax.experimental import pallas as pl
from jax.experimental.pallas import tpu as pltpu
from jax.sharding import PartitionSpec as P


DK = 128
C = 128
B = 256
SUB = 8
NN = (((1,), (0,)), ((), ()))
NT = (((1,), (1,)), ((), ()))
TN = (((0,), (0,)), ((), ()))


def partner(array, axis, stride):
    return lax.ppermute(array, axis, [(i, i ^ 1 << stride) for i in range(lax.axis_size(axis))])


def split(x):
    hi = x.astype(jnp.bfloat16)
    return hi, (x - hi.astype(jnp.float32)).astype(jnp.bfloat16)


def wide(parts):
    return jnp.concatenate(parts, axis=1)


def tall(parts):
    return jnp.concatenate(parts, axis=0)


def dot(a, b, dims):
    return lax.dot_general(a, b, dims, preferred_element_type=jnp.float32)


def halves(x):
    n = x.shape[1] // 2
    return x[:, :n] + x[:, n:]


def nn(a, b):
    right = wide(b)
    return halves(dot(wide(a), tall((right, right)), NN))


def nt(a, b):
    return halves(dot(wide(a), tall((wide((b[0], b[0])), wide((b[1], b[1])))), NT))


def tn(a, b):
    right = wide(b)
    return halves(dot(tall(a), tall((right, right)), TN))


def fold(x):
    return jnp.sum(x.reshape(x.shape[0] // SUB, SUB, x.shape[1]), axis=0)


def level_table():
    s = lax.broadcasted_iota(jnp.int32, (C, C), 0)
    t = lax.broadcasted_iota(jnp.int32, (C, C), 1)
    x = jnp.bitwise_xor(s, t)
    level = jnp.zeros((C, C), jnp.int32)
    for height in range(C.bit_length() - 1):
        level = level + (x >= 1 << height).astype(jnp.int32)
    return jnp.where(s <= t, level, -1)


def bit_of(level):
    return jnp.bitwise_and(jnp.right_shift(lax.axis_index("tm"), level), 1)


def halving_bit(level):
    return min(level, 2) - 1


def product(bit, row, turned, rights):
    grown = wide(split(jnp.where(bit == 1, row * turned[1], turned[0])))
    right = jnp.where(bit == 1, rights[1], rights[0])
    return dot(grown, tall((right, right)), NN)


def state_kernel(first, levels, k_hbm, q_hbm, v_hbm, d_hbm, w_hbm, send_refs, keep_refs, kq_ref, right_ref, turned_ref, flip_ref, w_ref, stage_ref, sum_ref, sems, w_sem):
    heads, frames = kq_ref.shape[1:3]
    half = heads // 2

    def copies(head):
        lanes = pl.ds(head * DK, DK)
        ends = (kq_ref.at[0, head], kq_ref.at[1, head], stage_ref.at[0, head], stage_ref.at[1, head])
        return [
            pltpu.make_async_copy(x.at[:, lanes], end, sems.at[i, head])
            for i, (x, end) in enumerate(zip((k_hbm, q_hbm, v_hbm, d_hbm), ends))
        ]

    def start(head):
        if head < heads:
            for copy in copies(head):
                copy.start()

    weights = pltpu.make_async_copy(w_hbm, w_ref, w_sem)
    weights.start()
    start(0)
    start(1)
    weights.wait()
    for head in range(heads):
        for copy in copies(head):
            copy.wait()
        start(head + 2)
        for b in range(frames // B):
            span = slice(b * B, (b + 1) * B)
            turned, rights = [], []
            for i in range(2):
                turned.append(kq_ref[i, head, span, :].T)
                rights.append(wide(split(stage_ref[i, head, span, :])))
                turned_ref[i, head, :, span] = turned[i]
                right_ref[i, head, span, :] = rights[i]
            for i, x in enumerate((turned[1], stage_ref[1, head, span, :].T)):
                for c in range(B // C):
                    flip_ref[i, head, b * (B // C) + c] = wide(split(x[:, c * C : (c + 1) * C]))
            for level in range(1, levels):
                row = w_ref[first + level : first + level + 1, span]
                term = product(bit_of(level), row, turned, rights)
                sum_ref[head, level - 1] = sum_ref[head, level - 1] + term if b else term
    for level in range(1, levels):
        own = bit_of(halving_bit(level))
        for j in range(half):
            low, high = halves(sum_ref[j, level - 1]), halves(sum_ref[half + j, level - 1])
            send_refs[level - 1][j] = jnp.where(own == 0, high, low)
            keep_refs[level - 1][j] = jnp.where(own == 0, low, high)


def near_kernel(first, right_ref, turned_ref, w_ref, near_ref):
    heads, frames = right_ref.shape[1:3]
    for head in range(heads):
        total = None
        for b in range(frames // B):
            span = slice(b * B, (b + 1) * B)
            turned = [turned_ref[i, head, :, span] for i in range(2)]
            rights = [right_ref[i, head, span, :] for i in range(2)]
            term = product(bit_of(0), w_ref[first : first + 1, span], turned, rights)
            total = term if total is None else total + term
        near_ref[head] = halves(total)


def upper_pairs(chunks):
    heights = chunks.bit_length() - 1
    return [(c, k) for c in range(chunks) for k in range(heights) if c >> k & 1]


def parts(ref, *at):
    x = ref[at]
    return x[:, :DK], x[:, DK:]


def local_kernel(heads, last, kq_ref, right_ref, turned_ref, flip_ref, w_ref, *refs):
    start = heads[0] == 0
    if not start:
        refs = refs[7:]
    qg_ref, kg_ref, vg_ref, pr_ref, wc_ref, mix_ref, col_ref = refs[:7]
    left_ref, me_ref, mg_ref = refs[-3:]
    frames = kq_ref.shape[2]
    chunks = frames // C
    heights = chunks.bit_length() - 1
    inner = C.bit_length()
    pairs = upper_pairs(chunks)
    spans = [slice(c * C, (c + 1) * C) for c in range(chunks)]

    if start:
        table = level_table()
        for c in range(chunks):
            mixing = jnp.zeros((C, C), jnp.float32)
            for level in range(inner):
                mixing = jnp.where(table == level, w_ref[level : level + 1, spans[c]], mixing)
            mix_ref[c] = mixing
            for i in range(col_ref.shape[0]):
                level = inner + heights + i
                col_ref[i, spans[c], :] = jnp.broadcast_to(w_ref[level : level + 1, spans[c]], (C, C)).T

    def right(i, head, span):
        return parts(right_ref, i, head, span)

    def add(head, ref, at, value):
        ref[at] = ref[at] + value if head else value

    def inside(head):
        lanes = slice(head * DK, (head + 1) * DK)
        sums, back = {}, {}
        place = head - heads[0]
        for c in range(chunks):
            for i in range(2):
                left_ref[place, i, spans[c], :] = wide(split(kq_ref[i, head, spans[c], :]))
        for c in range(chunks - 1):
            sums[c, 0] = tn(parts(left_ref, place, 0, spans[c]), right(0, head, spans[c]))
        for k in range(1, heights):
            for b in range(chunks >> k):
                if b << k < chunks - (1 << k):
                    sums[b, k] = sums[2 * b, k - 1] + sums[2 * b + 1, k - 1]

        def lefts(c):
            return parts(left_ref, place, 0, spans[c]), parts(left_ref, place, 1, spans[c])

        for c in range(chunks):
            ks, qs = lefts(c)
            gt = nn(ks, parts(flip_ref, 0, head, c))
            et = nn(right(0, head, spans[c]), parts(flip_ref, 1, head, c))
            add(head, pr_ref, c, gt * et)
            mt = mix_ref[c]
            me_ref[spans[c], :] = wide(split(mt * et))
            mg_ref[spans[c], :] = wide(split(mt * gt))
        for c in reversed(range(chunks)):
            ds = right(1, head, spans[c])
            qt = turned_ref[1, head, :, spans[c]]
            mixed = None
            for k in range(heights):
                if c >> k & 1:
                    row = w_ref[inner + k : inner + k + 1, spans[c]]
                    along = nn(split(sums[(c >> k) - 1, k]), parts(flip_ref, 1, head, c))
                    add(head, wc_ref, pairs.index((c, k)), fold(qt * along))
                    term = row * along
                    mixed = term if mixed is None else mixed + term
                    grad = nn(split(row * qt), ds)
                    key = ((c >> k) - 1, k)
                    back[key] = back[key] + grad if key in back else grad
            if mixed is not None:
                qg_ref[spans[c], lanes] = mixed.T
        for c in reversed(range(chunks)):
            ks, qs = lefts(c)
            vs, ds = right(0, head, spans[c]), right(1, head, spans[c])
            me, mg = parts(me_ref, spans[c]), parts(mg_ref, spans[c])
            kg, vg, qg = nn(me, qs), nn(mg, ds), tn(me, ks)
            if c < chunks - 1:
                total = None
                for k in range(heights):
                    if not c >> k & 1:
                        term = back[c >> k, k]
                        total = term if total is None else total + term
                bs = split(total)
                kg = kg + nt(vs, bs)
                vg = vg + nn(ks, bs)
            kg_ref[spans[c], lanes] = kg
            vg_ref[spans[c], lanes] = vg
            qg_ref[spans[c], lanes] = qg_ref[spans[c], lanes] + qg if c else qg

    for head in heads:
        inside(head)

    if last:
        wg_ref = refs[7]
        table = level_table()
        wg_ref[...] = jnp.zeros_like(wg_ref)
        for c in range(chunks):
            product = pr_ref[c]
            for level in range(inner):
                row = jnp.sum(jnp.where(table == level, product, 0.0), axis=0, keepdims=True)
                wg_ref[level : level + 1, spans[c]] = row
        for i, (c, k) in enumerate(pairs):
            wg_ref[inner + k : inner + k + 1, spans[c]] = jnp.sum(wc_ref[i], axis=0, keepdims=True)


def received(level, head, half, refs):
    if level == 0:
        return refs[0][head]
    other, mine = refs[2 * level - 1], refs[2 * level]
    return jnp.where(bit_of(halving_bit(level)) == head // half, mine[head % half], other[head % half])


def coarse_kernel(first, levels, kq_ref, right_ref, col_ref, old_q, old_w, *refs):
    arrived, (out_ref, wg_ref) = refs[:-2], refs[-2:]
    heads, frames = kq_ref.shape[1:3]
    arrived = [None] * (2 * levels[-1] + 1 - len(arrived)) + list(arrived)
    states = {}
    for head in range(heads):
        for level in levels:
            state = received(level, head, heads // 2, arrived)
            states[head, level] = split(jnp.where(bit_of(level) == 1, state, 0.0))
    for b in range(frames // B):
        span = slice(b * B, (b + 1) * B)
        products = {}
        for head in range(heads):
            lanes = slice(head * DK, (head + 1) * DK)
            ds = parts(right_ref, 1, head, span)
            q = kq_ref[1, head, span, :]
            mixed = old_q[span, lanes]
            for level in levels:
                along = nt(ds, states[head, level])
                share = q * along
                products[level] = products[level] + share if head else share
                mixed = mixed + col_ref[level, span, :] * along
            out_ref[span, lanes] = mixed
        for level in levels:
            row = jnp.sum(products[level].T, axis=0, keepdims=True)
            wg_ref[first + level : first + level + 1, span] = row


def back_kernel(levels, kq_ref, right_ref, old_k, old_v, q_ref, *refs):
    arrived = refs[: 2 * levels - 1]
    k_hbm, v_hbm, q_hbm, k_ref, v_ref, sems, q_sem = refs[2 * levels - 1 :]
    heads, frames = kq_ref.shape[1:3]
    blocks = frames // B
    queries = pltpu.make_async_copy(q_ref, q_hbm, q_sem)
    queries.start()

    def copies(head, b):
        at = (slice(b * B, (b + 1) * B), slice(head * DK, (head + 1) * DK))
        return [
            pltpu.make_async_copy(x.at[at], end.at[at], sems.at[i, head, b])
            for i, (x, end) in enumerate(((k_ref, k_hbm), (v_ref, v_hbm)))
        ]

    for head in range(heads):
        lanes = slice(head * DK, (head + 1) * DK)
        total = None
        for level in range(levels):
            state = received(level, head, heads // 2, arrived)
            term = jnp.where(bit_of(level) == 0, state, 0.0)
            total = term if total is None else total + term
        bs = split(total)
        for b in range(blocks):
            span = slice(b * B, (b + 1) * B)
            k_ref[span, lanes] = old_k[span, lanes] + nt(parts(right_ref, 0, head, span), bs)
            v_ref[span, lanes] = old_v[span, lanes] + nn(split(kq_ref[0, head, span, :]), bs)
            for copy in copies(head, b):
                copy.start()
    for head in range(heads):
        for b in range(blocks):
            for copy in copies(head, b):
                copy.wait()
    queries.wait()


def params(mib):
    return pltpu.CompilerParams(vmem_limit_bytes=mib * 2**20)


def cost(flops, size):
    return pl.CostEstimate(flops=flops, bytes_accessed=size, transcendentals=0)


def body(query_rows, key_rows, value_rows, out_grad, level_weights):
    frames, width = query_rows.shape
    heads = width // DK
    half = heads // 2
    levels = level_weights.shape[0]
    fine = frames.bit_length()
    device_levels = levels - fine
    far = device_levels - 1
    f32, bf16 = jnp.float32, jnp.bfloat16
    big = jax.ShapeDtypeStruct((frames, width), f32)
    kept = pltpu.VMEM((frames, width), f32)
    chunks = frames // C
    pairs = max(1, len(upper_pairs(chunks)))
    block = frames * width * 4
    here = pl.BlockSpec(memory_space=pltpu.VMEM)
    there = pl.BlockSpec(memory_space=pl.ANY)
    inputs = [pltpu.with_memory_space_constraint(x, pltpu.HBM) for x in (query_rows, key_rows, value_rows, out_grad, level_weights)]
    part = jax.ShapeDtypeStruct((half, DK, DK), f32)
    rows = -(-levels // SUB) * SUB

    send, keep, kq, right, turned, flip = pl.pallas_call(
        functools.partial(state_kernel, fine, device_levels),
        in_specs=[there] * 5,
        out_specs=[[here] * far] * 2 + [here] * 4,
        out_shape=[
            [part] * far,
            [part] * far,
            pltpu.VMEM((2, heads, frames, DK), f32),
            pltpu.VMEM((2, heads, frames, 2 * DK), bf16),
            pltpu.VMEM((2, heads, DK, frames), f32),
            pltpu.VMEM((2, heads, chunks, DK, 2 * C), bf16),
        ],
        scratch_shapes=[
            pltpu.VMEM((levels, frames), f32),
            pltpu.VMEM((2, heads, frames, DK), f32),
            pltpu.VMEM((heads, far, DK, 2 * DK), f32),
            pltpu.SemaphoreType.DMA((4, heads)),
            pltpu.SemaphoreType.DMA,
        ],
        compiler_params=params(16),
        cost_estimate=cost(10**9, 4 * block),
        name="states",
    )(inputs[1], inputs[0], *inputs[2:])

    near = pl.pallas_call(
        functools.partial(near_kernel, fine),
        in_specs=[here] * 3,
        out_specs=here,
        out_shape=jax.ShapeDtypeStruct((heads, DK, DK), f32),
        compiler_params=params(16),
        cost_estimate=cost(10**9, block),
        name="near",
    )(right, turned, level_weights)

    inner = None
    for head in range(heads):
        last = head == heads - 1
        shapes = [kept] * 3
        shapes += [pltpu.VMEM((chunks, C, C), f32), pltpu.VMEM((pairs, SUB, C), f32), pltpu.VMEM((chunks, C, C), f32)]
        shapes.append(pltpu.VMEM((device_levels, frames, DK), f32))
        if last:
            shapes.append(pltpu.VMEM((rows, frames), f32))
        inner = pl.pallas_call(
            functools.partial(local_kernel, [head], last),
            in_specs=[here] * (12 if head else 5),
            out_specs=[here] * len(shapes),
            out_shape=shapes,
            scratch_shapes=[pltpu.VMEM((1, 2, frames, 2 * DK), bf16)] + [pltpu.VMEM((frames, 2 * C), bf16)] * 2,
            input_output_aliases={5 + j: j for j in range(7)} if head else {},
            compiler_params=params(16),
            cost_estimate=cost(10**9, 7 * block // heads),
        )(kq, right, turned, flip, level_weights, *(inner or []))
    q_local, k_local, v_local, _, _, _, columns, weight_grad = inner

    states = [partner(near, "tm", 0)]
    for level in range(1, device_levels):
        halver = halving_bit(level)
        carried = keep[level - 1] + partner(send[level - 1], "tm", halver)
        for height in range(level):
            if height != halver:
                carried = carried + partner(carried, "tm", height)
        carried = partner(carried, "tm", level)
        states += [partner(carried, "tm", halver), carried]

    def coarse(span, query, weight):
        used = states[max(0, 2 * span[0] - 1) : 2 * span[-1] + 1]
        return pl.pallas_call(
            functools.partial(coarse_kernel, fine, span),
            in_specs=[here] * (5 + len(used)),
            out_specs=[here] * 2,
            out_shape=[kept, pltpu.VMEM((rows, frames), f32)],
            input_output_aliases={3: 0, 4: 1},
            compiler_params=params(16),
            cost_estimate=cost(10**9, 2 * block),
            name="coarse",
        )(kq, right, columns, query, weight, *used)

    q_local, weight_grad = coarse(list(range(far)), q_local, weight_grad)
    q_local, weight_grad = coarse([far], q_local, weight_grad)
    for height in range(lax.axis_size("head").bit_length() - 1):
        weight_grad = weight_grad + partner(weight_grad, "head", height)

    k_total, v_total, q_total = pl.pallas_call(
        functools.partial(back_kernel, device_levels),
        in_specs=[here] * (5 + len(states)),
        out_specs=[there] * 3,
        out_shape=[big] * 3,
        scratch_shapes=[
            pltpu.VMEM((frames, width), f32),
            pltpu.VMEM((frames, width), f32),
            pltpu.SemaphoreType.DMA((2, heads, frames // B)),
            pltpu.SemaphoreType.DMA,
        ],
        compiler_params=params(16),
        cost_estimate=cost(10**9, 4 * block),
        name="back",
    )(kq, right, k_local, v_local, q_local, *states)
    return (q_total, k_total, v_total, weight_grad[:levels])


def solution(mesh):
    in_specs = (P("tm", "head"), P("tm", "head"), P("tm", "head"), P("tm", "head"), P(None, "tm"))
    out_specs = (P("tm", "head"), P("tm", "head"), P("tm", "head"), P(None, "tm"))
    return jax.shard_map(body, mesh=mesh, in_specs=in_specs, out_specs=out_specs, check_vma=False)
```

```python
import functools

import jax
import jax.numpy as jnp
from jax import lax
from jax.experimental import pallas as pl
from jax.experimental.pallas import tpu as pltpu
from jax.sharding import PartitionSpec as P


DK = 128
C = 128
B = 256
SUB = 8
NN = (((1,), (0,)), ((), ()))
NT = (((1,), (1,)), ((), ()))
TN = (((0,), (0,)), ((), ()))


def partner(array, axis, stride):
    return lax.ppermute(array, axis, [(i, i ^ 1 << stride) for i in range(lax.axis_size(axis))])


def split(x):
    hi = x.astype(jnp.bfloat16)
    return hi, (x - hi.astype(jnp.float32)).astype(jnp.bfloat16)


def wide(parts):
    return jnp.concatenate(parts, axis=1)


def tall(parts):
    return jnp.concatenate(parts, axis=0)


def dot(a, b, dims):
    return lax.dot_general(a, b, dims, preferred_element_type=jnp.float32)


def halves(x):
    n = x.shape[1] // 2
    return x[:, :n] + x[:, n:]


def nn(a, b):
    right = wide(b)
    return halves(dot(wide(a), tall((right, right)), NN))


def nt(a, b):
    return halves(dot(wide(a), tall((wide((b[0], b[0])), wide((b[1], b[1])))), NT))


def tn(a, b):
    right = wide(b)
    return halves(dot(tall(a), tall((right, right)), TN))


def fold(x):
    return jnp.sum(x.reshape(x.shape[0] // SUB, SUB, x.shape[1]), axis=0)


def level_table():
    s = lax.broadcasted_iota(jnp.int32, (C, C), 0)
    t = lax.broadcasted_iota(jnp.int32, (C, C), 1)
    x = jnp.bitwise_xor(s, t)
    level = jnp.zeros((C, C), jnp.int32)
    for height in range(C.bit_length() - 1):
        level = level + (x >= 1 << height).astype(jnp.int32)
    return jnp.where(s <= t, level, -1)


def bit_of(level):
    return jnp.bitwise_and(jnp.right_shift(lax.axis_index("tm"), level), 1)


def halving_bit(level):
    return min(level, 2) - 1


def product(bit, row, turned, rights):
    grown = wide(split(jnp.where(bit == 1, row * turned[1], turned[0])))
    right = jnp.where(bit == 1, rights[1], rights[0])
    return dot(grown, tall((right, right)), NN)


def state_kernel(first, levels, k_hbm, q_hbm, v_hbm, d_hbm, w_hbm, send_refs, keep_refs, kq_ref, right_ref, turned_ref, w_ref, stage_ref, sum_ref, sems, w_sem):
    heads, frames = kq_ref.shape[1:3]
    half = heads // 2

    def copies(head):
        lanes = pl.ds(head * DK, DK)
        ends = (kq_ref.at[0, head], kq_ref.at[1, head], stage_ref.at[0, head], stage_ref.at[1, head])
        return [
            pltpu.make_async_copy(x.at[:, lanes], end, sems.at[i, head])
            for i, (x, end) in enumerate(zip((k_hbm, q_hbm, v_hbm, d_hbm), ends))
        ]

    def start(head):
        if head < heads:
            for copy in copies(head):
                copy.start()

    weights = pltpu.make_async_copy(w_hbm, w_ref, w_sem)
    weights.start()
    start(0)
    start(1)
    weights.wait()
    for head in range(heads):
        for copy in copies(head):
            copy.wait()
        start(head + 2)
        for b in range(frames // B):
            span = slice(b * B, (b + 1) * B)
            turned, rights = [], []
            for i in range(2):
                turned.append(kq_ref[i, head, span, :].T)
                rights.append(wide(split(stage_ref[i, head, span, :])))
                turned_ref[i, head, :, span] = turned[i]
                right_ref[i, head, span, :] = rights[i]
            for level in range(1, levels):
                row = w_ref[first + level : first + level + 1, span]
                term = product(bit_of(level), row, turned, rights)
                sum_ref[head, level - 1] = sum_ref[head, level - 1] + term if b else term
    for level in range(1, levels):
        own = bit_of(halving_bit(level))
        for j in range(half):
            low, high = halves(sum_ref[j, level - 1]), halves(sum_ref[half + j, level - 1])
            send_refs[level - 1][j] = jnp.where(own == 0, high, low)
            keep_refs[level - 1][j] = jnp.where(own == 0, low, high)


def near_kernel(first, right_ref, turned_ref, w_ref, near_ref):
    heads, frames = right_ref.shape[1:3]
    for head in range(heads):
        total = None
        for b in range(frames // B):
            span = slice(b * B, (b + 1) * B)
            turned = [turned_ref[i, head, :, span] for i in range(2)]
            rights = [right_ref[i, head, span, :] for i in range(2)]
            term = product(bit_of(0), w_ref[first : first + 1, span], turned, rights)
            total = term if total is None else total + term
        near_ref[head] = halves(total)


def upper_pairs(chunks):
    heights = chunks.bit_length() - 1
    return [(c, k) for c in range(chunks) for k in range(heights) if c >> k & 1]


def parts(ref, *at):
    x = ref[at]
    return x[:, :DK], x[:, DK:]


def local_kernel(heads, last, kq_ref, right_ref, turned_ref, w_ref, *refs):
    start = heads[0] == 0
    if not start:
        refs = refs[7:]
    qg_ref, kg_ref, vg_ref, pr_ref, wc_ref, mix_ref, col_ref = refs[:7]
    left_ref, me_ref, mg_ref, flip_ref = refs[-4:]
    frames = kq_ref.shape[2]
    chunks = frames // C
    heights = chunks.bit_length() - 1
    inner = C.bit_length()
    pairs = upper_pairs(chunks)
    spans = [slice(c * C, (c + 1) * C) for c in range(chunks)]

    if start:
        table = level_table()
        for c in range(chunks):
            mixing = jnp.zeros((C, C), jnp.float32)
            for level in range(inner):
                mixing = jnp.where(table == level, w_ref[level : level + 1, spans[c]], mixing)
            mix_ref[c] = mixing
            for i in range(col_ref.shape[0]):
                level = inner + heights + i
                col_ref[i, spans[c], :] = jnp.broadcast_to(w_ref[level : level + 1, spans[c]], (C, C)).T

    def right(i, head, span):
        return parts(right_ref, i, head, span)

    def add(head, ref, at, value):
        ref[at] = ref[at] + value if head else value

    def inside(head):
        lanes = slice(head * DK, (head + 1) * DK)
        sums, back = {}, {}
        place = head - heads[0]
        for c in range(chunks):
            for i in range(2):
                left_ref[place, i, spans[c], :] = wide(split(kq_ref[i, head, spans[c], :]))
            flip_ref[0, c] = wide(split(turned_ref[1, head, :, spans[c]]))
            flip_ref[1, c] = wide([x.T for x in right(1, head, spans[c])])
        for c in range(chunks - 1):
            sums[c, 0] = tn(parts(left_ref, place, 0, spans[c]), right(0, head, spans[c]))
        for k in range(1, heights):
            for b in range(chunks >> k):
                if b << k < chunks - (1 << k):
                    sums[b, k] = sums[2 * b, k - 1] + sums[2 * b + 1, k - 1]

        def lefts(c):
            return parts(left_ref, place, 0, spans[c]), parts(left_ref, place, 1, spans[c])

        for c in range(chunks):
            ks, qs = lefts(c)
            gt = nn(ks, parts(flip_ref, 0, c))
            et = nn(right(0, head, spans[c]), parts(flip_ref, 1, c))
            add(head, pr_ref, c, gt * et)
            mt = mix_ref[c]
            me_ref[spans[c], :] = wide(split(mt * et))
            mg_ref[spans[c], :] = wide(split(mt * gt))
        for c in reversed(range(chunks)):
            ds = right(1, head, spans[c])
            qt = turned_ref[1, head, :, spans[c]]
            mixed = None
            for k in range(heights):
                if c >> k & 1:
                    row = w_ref[inner + k : inner + k + 1, spans[c]]
                    along = nn(split(sums[(c >> k) - 1, k]), parts(flip_ref, 1, c))
                    add(head, wc_ref, pairs.index((c, k)), fold(qt * along))
                    term = row * along
                    mixed = term if mixed is None else mixed + term
                    grad = nn(split(row * qt), ds)
                    key = ((c >> k) - 1, k)
                    back[key] = back[key] + grad if key in back else grad
            if mixed is not None:
                qg_ref[spans[c], lanes] = mixed.T
        for c in reversed(range(chunks)):
            ks, qs = lefts(c)
            vs, ds = right(0, head, spans[c]), right(1, head, spans[c])
            me, mg = parts(me_ref, spans[c]), parts(mg_ref, spans[c])
            kg, vg, qg = nn(me, qs), nn(mg, ds), tn(me, ks)
            if c < chunks - 1:
                total = None
                for k in range(heights):
                    if not c >> k & 1:
                        term = back[c >> k, k]
                        total = term if total is None else total + term
                bs = split(total)
                kg = kg + nt(vs, bs)
                vg = vg + nn(ks, bs)
            kg_ref[spans[c], lanes] = kg
            vg_ref[spans[c], lanes] = vg
            qg_ref[spans[c], lanes] = qg_ref[spans[c], lanes] + qg if c else qg

    for head in heads:
        inside(head)

    if last:
        wg_ref = refs[7]
        table = level_table()
        wg_ref[...] = jnp.zeros_like(wg_ref)
        for c in range(chunks):
            product = pr_ref[c]
            for level in range(inner):
                row = jnp.sum(jnp.where(table == level, product, 0.0), axis=0, keepdims=True)
                wg_ref[level : level + 1, spans[c]] = row
        for i, (c, k) in enumerate(pairs):
            wg_ref[inner + k : inner + k + 1, spans[c]] = jnp.sum(wc_ref[i], axis=0, keepdims=True)


def received(level, head, half, refs):
    if level == 0:
        return refs[0][head]
    other, mine = refs[2 * level - 1], refs[2 * level]
    return jnp.where(bit_of(halving_bit(level)) == head // half, mine[head % half], other[head % half])


def coarse_kernel(first, levels, kq_ref, right_ref, col_ref, old_q, old_w, *refs):
    arrived, (out_ref, wg_ref) = refs[:-2], refs[-2:]
    heads, frames = kq_ref.shape[1:3]
    arrived = [None] * (2 * levels[-1] + 1 - len(arrived)) + list(arrived)
    states = {}
    for head in range(heads):
        for level in levels:
            state = received(level, head, heads // 2, arrived)
            states[head, level] = split(jnp.where(bit_of(level) == 1, state, 0.0))
    for b in range(frames // B):
        span = slice(b * B, (b + 1) * B)
        products = {}
        for head in range(heads):
            lanes = slice(head * DK, (head + 1) * DK)
            ds = parts(right_ref, 1, head, span)
            q = kq_ref[1, head, span, :]
            mixed = old_q[span, lanes]
            for level in levels:
                along = nt(ds, states[head, level])
                share = q * along
                products[level] = products[level] + share if head else share
                mixed = mixed + col_ref[level, span, :] * along
            out_ref[span, lanes] = mixed
        for level in levels:
            row = jnp.sum(products[level].T, axis=0, keepdims=True)
            wg_ref[first + level : first + level + 1, span] = row


def back_kernel(levels, kq_ref, right_ref, old_k, old_v, q_ref, *refs):
    arrived = refs[: 2 * levels - 1]
    k_hbm, v_hbm, q_hbm, k_ref, v_ref, sems, q_sem = refs[2 * levels - 1 :]
    heads, frames = kq_ref.shape[1:3]
    blocks = frames // B
    queries = pltpu.make_async_copy(q_ref, q_hbm, q_sem)
    queries.start()

    def copies(head, b):
        at = (slice(b * B, (b + 1) * B), slice(head * DK, (head + 1) * DK))
        return [
            pltpu.make_async_copy(x.at[at], end.at[at], sems.at[i, head, b])
            for i, (x, end) in enumerate(((k_ref, k_hbm), (v_ref, v_hbm)))
        ]

    for head in range(heads):
        lanes = slice(head * DK, (head + 1) * DK)
        total = None
        for level in range(levels):
            state = received(level, head, heads // 2, arrived)
            term = jnp.where(bit_of(level) == 0, state, 0.0)
            total = term if total is None else total + term
        bs = split(total)
        for b in range(blocks):
            span = slice(b * B, (b + 1) * B)
            k_ref[span, lanes] = old_k[span, lanes] + nt(parts(right_ref, 0, head, span), bs)
            v_ref[span, lanes] = old_v[span, lanes] + nn(split(kq_ref[0, head, span, :]), bs)
            for copy in copies(head, b):
                copy.start()
    for head in range(heads):
        for b in range(blocks):
            for copy in copies(head, b):
                copy.wait()
    queries.wait()


def params(mib):
    return pltpu.CompilerParams(vmem_limit_bytes=mib * 2**20)


def cost(flops, size):
    return pl.CostEstimate(flops=flops, bytes_accessed=size, transcendentals=0)


def body(query_rows, key_rows, value_rows, out_grad, level_weights):
    frames, width = query_rows.shape
    heads = width // DK
    half = heads // 2
    levels = level_weights.shape[0]
    fine = frames.bit_length()
    device_levels = levels - fine
    far = device_levels - 1
    f32, bf16 = jnp.float32, jnp.bfloat16
    big = jax.ShapeDtypeStruct((frames, width), f32)
    kept = pltpu.VMEM((frames, width), f32)
    chunks = frames // C
    pairs = max(1, len(upper_pairs(chunks)))
    block = frames * width * 4
    here = pl.BlockSpec(memory_space=pltpu.VMEM)
    there = pl.BlockSpec(memory_space=pl.ANY)
    inputs = [pltpu.with_memory_space_constraint(x, pltpu.HBM) for x in (query_rows, key_rows, value_rows, out_grad, level_weights)]
    part = jax.ShapeDtypeStruct((half, DK, DK), f32)
    rows = -(-levels // SUB) * SUB

    send, keep, kq, right, turned = pl.pallas_call(
        functools.partial(state_kernel, fine, device_levels),
        in_specs=[there] * 5,
        out_specs=[[here] * far] * 2 + [here] * 3,
        out_shape=[
            [part] * far,
            [part] * far,
            pltpu.VMEM((2, heads, frames, DK), f32),
            pltpu.VMEM((2, heads, frames, 2 * DK), bf16),
            pltpu.VMEM((2, heads, DK, frames), f32),
        ],
        scratch_shapes=[
            pltpu.VMEM((levels, frames), f32),
            pltpu.VMEM((2, heads, frames, DK), f32),
            pltpu.VMEM((heads, far, DK, 2 * DK), f32),
            pltpu.SemaphoreType.DMA((4, heads)),
            pltpu.SemaphoreType.DMA,
        ],
        compiler_params=params(16),
        cost_estimate=cost(10**9, 4 * block),
        name="states",
    )(inputs[1], inputs[0], *inputs[2:])

    near = pl.pallas_call(
        functools.partial(near_kernel, fine),
        in_specs=[here] * 3,
        out_specs=here,
        out_shape=jax.ShapeDtypeStruct((heads, DK, DK), f32),
        compiler_params=params(16),
        cost_estimate=cost(10**9, block),
        name="near",
    )(right, turned, level_weights)

    inner = None
    for head in range(heads):
        last = head == heads - 1
        shapes = [kept] * 3
        shapes += [pltpu.VMEM((chunks, C, C), f32), pltpu.VMEM((pairs, SUB, C), f32), pltpu.VMEM((chunks, C, C), f32)]
        shapes.append(pltpu.VMEM((device_levels, frames, DK), f32))
        if last:
            shapes.append(pltpu.VMEM((rows, frames), f32))
        inner = pl.pallas_call(
            functools.partial(local_kernel, [head], last),
            in_specs=[here] * (11 if head else 4),
            out_specs=[here] * len(shapes),
            out_shape=shapes,
            scratch_shapes=[pltpu.VMEM((1, 2, frames, 2 * DK), bf16)]
            + [pltpu.VMEM((frames, 2 * C), bf16)] * 2
            + [pltpu.VMEM((2, chunks, DK, 2 * C), bf16)],
            input_output_aliases={4 + j: j for j in range(7)} if head else {},
            compiler_params=params(16),
            cost_estimate=cost(10**9, 7 * block // heads),
        )(kq, right, turned, level_weights, *(inner or []))
    q_local, k_local, v_local, _, _, _, columns, weight_grad = inner

    states = [partner(near, "tm", 0)]
    for level in range(1, device_levels):
        halver = halving_bit(level)
        carried = keep[level - 1] + partner(send[level - 1], "tm", halver)
        for height in range(level):
            if height != halver:
                carried = carried + partner(carried, "tm", height)
        carried = partner(carried, "tm", level)
        states += [partner(carried, "tm", halver), carried]

    def coarse(span, query, weight):
        used = states[max(0, 2 * span[0] - 1) : 2 * span[-1] + 1]
        return pl.pallas_call(
            functools.partial(coarse_kernel, fine, span),
            in_specs=[here] * (5 + len(used)),
            out_specs=[here] * 2,
            out_shape=[kept, pltpu.VMEM((rows, frames), f32)],
            input_output_aliases={3: 0, 4: 1},
            compiler_params=params(16),
            cost_estimate=cost(10**9, 2 * block),
            name="coarse",
        )(kq, right, columns, query, weight, *used)

    q_local, weight_grad = coarse(list(range(far)), q_local, weight_grad)
    q_local, weight_grad = coarse([far], q_local, weight_grad)
    for height in range(lax.axis_size("head").bit_length() - 1):
        weight_grad = weight_grad + partner(weight_grad, "head", height)

    k_total, v_total, q_total = pl.pallas_call(
        functools.partial(back_kernel, device_levels),
        in_specs=[here] * (5 + len(states)),
        out_specs=[there] * 3,
        out_shape=[big] * 3,
        scratch_shapes=[
            pltpu.VMEM((frames, width), f32),
            pltpu.VMEM((frames, width), f32),
            pltpu.SemaphoreType.DMA((2, heads, frames // B)),
            pltpu.SemaphoreType.DMA,
        ],
        compiler_params=params(16),
        cost_estimate=cost(10**9, 4 * block),
        name="back",
    )(kq, right, k_local, v_local, q_local, *states)
    return (q_total, k_total, v_total, weight_grad[:levels])


def solution(mesh):
    in_specs = (P("tm", "head"), P("tm", "head"), P("tm", "head"), P("tm", "head"), P(None, "tm"))
    out_specs = (P("tm", "head"), P("tm", "head"), P("tm", "head"), P(None, "tm"))
    return jax.shard_map(body, mesh=mesh, in_specs=in_specs, out_specs=out_specs, check_vma=False)
```
